512 devices in a mesh: ctx: 32 (over z, x_lo), zero: 16 (over x_hi, y, core).
Axes of the slice: x: 4 (x_hi: 2, x_lo: 2; x = x_hi * 2 + x_lo), y: 4, z: 16, core: 2. Of those that a mesh axis runs over, the one named last changes fastest.
Arguments:
- activations: bfloat16 [16384, 4096], P('ctx', 'zero'), may hold values from -1200 to 1200
- norm_gain: bfloat16 [4096], replicated, may hold values from 0.099609375 to 1.8984375
- query_weight: bfloat16 [4096, 4096], P('ctx', 'zero'), may hold values from -24 to 24
- kv_weight: bfloat16 [4096, 16, 128], P('ctx', 'zero'), may hold values from -1 to 1
- out_weight: bfloat16 [4096, 4096], P('zero', 'ctx'), may hold values from -0.09375 to 0.09375
- tile_mask: int32 [32, 4, 4], P('ctx'), may hold values from 0 to 1, as said below
- anchor_mask: int32 [32, 4, 4], P('ctx'), may hold values 0 or 1
- anchor_index: int32 [1], replicated, may hold values from 0 to 31
Outputs:
- mixed: bfloat16 [16384, 4096], P(('ctx', 'zero'))
The draws below stay inside these ranges and needn't reach their ends.
Inputs may be any that keep to these rules, and one draw needn't show every extreme that they name: `tile_mask`: entries of every block's table above the diagonal are 0 and diagonal entries are 1.
All inputs are finite; a program needn't handle non-finite values. No bound on the sum of `anchor_mask` on one device may be relied on, other than what follows from the above.
Results may differ from the reference program's by a relative error of at most 0.02.
Values may be sent and summed in bfloat16 or wider, within the bound.
A program may use at most 64 MiB of HBM per device.

```python
import math
import jax
import jax.numpy as jnp
from jax import lax

D = 4096
HD = 128
QH_DEV = 2
TILE = 128
BLOCK = 512
HQ = 32
KVH = 8
BLOCKS = 32
TOKENS = 16384
NT = 4


def key_base(key):
    return jnp.clip(jax.random.normal(jax.random.fold_in(key, 11), (D, KVH, HD), jnp.float32), -6.0, 6.0) * D ** (-0.5)


def draw_activations(key, part):
    first, second, third = jax.random.split(key, 3)
    row_scale = jnp.exp(jax.random.uniform(second, (TOKENS, 1), jnp.float32) * math.log(10.0))
    column_scale = jnp.exp(jax.random.uniform(third, (1, D), jnp.float32) * math.log(10.0))
    base = jnp.clip(jax.random.normal(first, (TOKENS, D), jnp.float32), -6.0, 6.0)
    return (base * row_scale * column_scale).astype(jnp.bfloat16)


def draw_query_weight(key, part):
    drawn = jnp.clip(jax.random.normal(jax.random.fold_in(key, 12), (D, HQ, HD), jnp.float32), -6.0, 6.0) * D ** (-0.5)
    return drawn.reshape(D, HQ * HD).astype(jnp.bfloat16)


def draw_kv_weight(key, part):
    key_part = key_base(key)
    value_part = jnp.clip(jax.random.normal(jax.random.fold_in(key, 14), (D, KVH, HD), jnp.float32), -6.0, 6.0) * D ** (-0.5)
    return jnp.stack([key_part, value_part], axis=2).reshape(D, 2 * KVH, HD).astype(jnp.bfloat16)


def draw_tile_mask(key, part):
    coins = jax.random.randint(key, (BLOCKS, NT, NT), 0, 2, jnp.int32)
    lower = jnp.tril(coins, -1)
    return lower + jnp.eye(NT, dtype=jnp.int32)[None]


def with_ends(array, rng, smallest, high):
    longest = array.shape.index(max(array.shape))
    spots = []
    for shift in (0, 1):
        where = [jax.random.randint(jax.random.fold_in(rng, axis), (), 0, length) for axis, length in enumerate(array.shape)]
        where[longest] = (where[longest] + shift) % array.shape[longest]
        spots.append(tuple(where))
    return array.at[spots[0]].set(smallest).at[spots[1]].set(high)


def shard_levels(stream_key, shape, cuts, least, high):
    loudness, own = 1.0, jax.random.fold_in(stream_key, 6)
    for position, parts in cuts:
        draws = jnp.exp(jax.random.uniform(jax.random.fold_in(own, position), (parts,), jnp.float32, least / len(cuts), high / len(cuts)))
        loudness = loudness * jnp.repeat(draws, shape[position] // parts).reshape([-1 if axis == position else 1 for axis in range(len(shape))])
    return loudness


def noise(stream_key, shape, spread, bound, shards=(), held_as=jnp.bfloat16):
    drawn = jax.random.normal(stream_key, shape, jnp.float32) * spread
    if len(shards) > 0:
        drawn = shard_levels(stream_key, shape, shards, -0.22, 0.18) * drawn
    return jnp.clip(drawn, min=-bound, max=bound).astype(held_as)


def setup_inputs(seed: int = 0) -> dict:
    seeds = jax.random.split(jax.random.key(seed), 9)
    activations = draw_activations(jax.random.fold_in(seeds[8], 71), 0)
    norm_gain = jnp.clip(1.0 + 0.18 * jax.random.normal(seeds[1], (D,), jnp.float32), 0.099609375, 1.8984375).astype(jnp.bfloat16)
    query_weight = draw_query_weight(jax.random.fold_in(seeds[8], 71), 0)
    kv_weight = draw_kv_weight(jax.random.fold_in(seeds[8], 71), 0)
    out_weight = noise(seeds[4], (HQ * HD, D), (HQ * HD) ** -0.5, 0.09375, ((0, 16), (1, 32)))
    tile_mask = draw_tile_mask(jax.random.fold_in(seeds[8], 71), 0)
    anchor_mask = with_ends((jax.random.randint(seeds[6], (BLOCKS, NT, NT), 0, 4) < 3).astype(jnp.int32), jax.random.fold_in(seeds[6], 1), 0, 1)
    anchor_index = jax.random.randint(seeds[7], (1,), 0, BLOCKS).astype(jnp.int32)
    return dict(activations=activations, norm_gain=norm_gain, query_weight=query_weight, kv_weight=kv_weight, out_weight=out_weight, tile_mask=tile_mask, anchor_mask=anchor_mask, anchor_index=anchor_index)


def rotate(vectors, positions):
    half_size = vectors.shape[-1] // 2
    frequency = jnp.power(jnp.float32(500000.0), -(jnp.arange(half_size, dtype=jnp.float32) * 2.0 / vectors.shape[-1]))
    angles = positions.astype(jnp.float32)[:, None] * frequency[None, :]
    cosine_table = jnp.cos(angles)[:, None, :]
    sine_table = jnp.sin(angles)[:, None, :]
    first = vectors[..., :half_size]
    second = vectors[..., half_size:]
    return jnp.concatenate([first * cosine_table - second * sine_table, second * cosine_table + first * sine_table], -1)

def expand_tiles(table):
    tiles = table.shape[0]
    return jnp.broadcast_to(table[:, None, :, None], (tiles, TILE, tiles, TILE)).reshape(tiles * TILE, tiles * TILE)

def reference(activations, norm_gain, query_weight, kv_weight, out_weight, tile_mask, anchor_mask, anchor_index):
    x_float = activations.astype(jnp.float32)
    mean_square = lax.optimization_barrier(jnp.mean(x_float * x_float, -1, keepdims=True))
    normed = (x_float * lax.rsqrt(mean_square + 1e-05) * norm_gain.astype(jnp.float32)).astype(jnp.bfloat16)
    positions = jnp.arange(TOKENS, dtype=jnp.int32)
    queries = (rotate(jnp.dot(normed, query_weight, preferred_element_type=jnp.float32).reshape(TOKENS, HQ, HD), positions) * HD ** (-0.5)).astype(jnp.bfloat16)
    key_weight = kv_weight[:, 0::2, :].reshape(D, KVH * HD)
    value_weight = kv_weight[:, 1::2, :].reshape(D, KVH * HD)
    keys = rotate(jnp.dot(normed, key_weight, preferred_element_type=jnp.float32).reshape(TOKENS, KVH, HD), positions).astype(jnp.bfloat16)
    values = jnp.dot(normed, value_weight, preferred_element_type=jnp.float32).astype(jnp.bfloat16).reshape(TOKENS, KVH, HD)
    anchor_block = anchor_index[0]
    group_size = HQ // KVH
    row_offsets = jnp.arange(BLOCK, dtype=jnp.int32)

    def host(host_index):
        host_queries = lax.dynamic_slice_in_dim(queries, host_index * BLOCK, BLOCK, 0).astype(jnp.float32)
        all_keys = jnp.concatenate([lax.dynamic_slice_in_dim(keys, anchor_block * BLOCK, BLOCK, 0), lax.dynamic_slice_in_dim(keys, host_index * BLOCK, BLOCK, 0)], 0)
        all_values = jnp.concatenate([lax.dynamic_slice_in_dim(values, anchor_block * BLOCK, BLOCK, 0), lax.dynamic_slice_in_dim(values, host_index * BLOCK, BLOCK, 0)], 0)
        all_keys = jnp.repeat(all_keys.astype(jnp.float32), group_size, axis=1)
        all_values = jnp.repeat(all_values.astype(jnp.float32), group_size, axis=1)
        scores = jnp.einsum('thd,khd->htk', host_queries, all_keys)
        far_visible = (expand_tiles(anchor_mask[host_index]) == 1) & (host_index != anchor_block)
        near_visible = (expand_tiles(tile_mask[host_index]) == 1) & (row_offsets[None, :] <= row_offsets[:, None])
        visible = jnp.concatenate([far_visible, near_visible], 1)[None]
        scores = jnp.where(visible, scores, jnp.float32(-1e+30))
        largest = lax.optimization_barrier(jnp.max(scores, -1, keepdims=True))
        weights = jnp.where(visible, jnp.exp(scores - largest), jnp.float32(0.0))
        row_total = lax.optimization_barrier(jnp.sum(weights, -1))
        rounded = lax.optimization_barrier(weights.astype(jnp.bfloat16)).astype(jnp.float32)
        attended = jnp.einsum('htk,khd->thd', rounded, all_values) / jnp.transpose(row_total)[:, :, None]
        return attended.astype(jnp.bfloat16).reshape(BLOCK, HQ * HD)
    attended = lax.map(host, jnp.arange(BLOCKS, dtype=jnp.int32)).reshape(TOKENS, HQ * HD)
    group_width = QH_DEV * HD

    def add_group(running, group_index):
        columns = lax.dynamic_slice_in_dim(attended, group_index * group_width, group_width, 1)
        weight_rows = lax.dynamic_slice_in_dim(out_weight, group_index * group_width, group_width, 0)
        group_term = jnp.dot(columns, weight_rows, preferred_element_type=jnp.float32)
        group_term = lax.optimization_barrier(group_term.astype(jnp.bfloat16)).astype(jnp.float32)
        return (running + group_term, None)
    running = lax.scan(add_group, jnp.zeros((TOKENS, D), jnp.float32), jnp.arange(HQ // QH_DEV, dtype=jnp.int32))[0]
    return running.astype(jnp.bfloat16)
```

```python
import functools

import numpy as np

import jax
import jax.numpy as jnp
from jax import lax
from jax.experimental import pallas as pl
from jax.experimental.pallas import tpu as pltpu
from jax.sharding import PartitionSpec as P

MESH = pl.DeviceIdType.MESH
F32 = jnp.float32
BF16 = jnp.bfloat16
MASKED = -1e30
UNITS = 8
LAG = 1

ORDER_HOME = [
    ("A", 0, 0, 0), ("A", 0, 0, 1), ("B", 0, 0, 0), ("B", 0, 0, 1), ("A", 0, 3, 0), ("A", 0, 1, 0),
    ("A", 0, 3, 1), ("A", 0, 1, 1), ("B", 0, 3, 0), ("B", 0, 1, 0), ("B", 0, 3, 1), ("B", 0, 1, 1),
    ("A", 0, 2, 0), ("A", 2, 0, 0), ("A", 2, 0, 1), ("B", 2, 0, 0), ("A", 0, 2, 1), ("B", 0, 2, 0),
    ("B", 0, 2, 1), ("B", 2, 0, 1), ("A", 2, 3, 0), ("A", 2, 1, 0), ("B", 2, 3, 0), ("B", 2, 3, 1),
    ("A", 2, 3, 1), ("A", 2, 1, 1), ("B", 2, 1, 0), ("B", 2, 1, 1), ("A", 2, 2, 0), ("A", 2, 2, 1),
    ("B", 2, 2, 0), ("B", 2, 2, 1),
]
ORDER_AWAY = [
    ("A", 1, 0, 0), ("A", 3, 0, 0), ("A", 1, 0, 1), ("A", 3, 0, 1), ("B", 1, 0, 0), ("B", 3, 0, 0),
    ("B", 1, 0, 1), ("B", 3, 0, 1), ("A", 1, 3, 0), ("A", 1, 1, 0), ("A", 3, 3, 0), ("B", 1, 3, 0),
    ("B", 3, 3, 0), ("A", 3, 1, 0), ("A", 1, 3, 1), ("B", 1, 1, 0), ("B", 3, 1, 0), ("A", 1, 1, 1),
    ("B", 3, 3, 1), ("A", 3, 3, 1), ("A", 3, 1, 1), ("B", 1, 3, 1), ("B", 3, 1, 1), ("B", 1, 1, 1),
    ("A", 1, 2, 0), ("B", 3, 2, 0), ("A", 1, 2, 1), ("B", 1, 2, 0), ("B", 3, 2, 1), ("A", 3, 2, 0),
    ("A", 3, 2, 1), ("B", 1, 2, 1),
]
STEPS = [(1, 0), (-1, 0), (0, 1), (0, -1)]
XP, XM, YP, YM = range(4)


def onward(kind, dx, dy, half):
    first, second = (dx, dy) if kind == "A" else (dy, dx)
    fp, fm, sp, sm = (XP, XM, YP, YM) if kind == "A" else (YP, YM, XP, XM)
    ways = []
    if second == 0:
        if first == 0:
            ways += [fp, fm]
        if first == 1 and half == 0:
            ways += [fp]
        if first == 3 and half == 1:
            ways += [fm]
        ways += [sp, sm]
    if second == 1 and half == 0:
        ways += [sp]
    if second == 3 and half == 1:
        ways += [sm]
    return ways


def body(
    acts, gain, wq, wkv, wo, tmask, amask, aidx, ctab, stab, coff, soff, out,
    X, WQ, WKV, WO, ACCQ, ACCK, SSQ, QB, KV, TMR, AMR, BOWN, BFAR,
    AB, CAND, AR, SEL, AKV, MS, LS, ACC, ATT, PB, RX, RYC, RYF, SB, OB,
    rx, sx, sd, loc, r0kv, r0q, r0o, s0, rz, sz, rs, ss, rm, sm,
    ra, sa, rar, sar, rak, sak, rad, sad,
    rpx, spx, rpyc, rpyf, spy, rpd, spd,
):
    ctx = lax.axis_index("ctx")
    zero = lax.axis_index("zero")
    z, xl = lax.div(ctx, 2), lax.rem(ctx, 2)
    xh, y, core = lax.div(zero, 8), lax.rem(lax.div(zero, 2), 4), lax.rem(zero, 2)
    x = 2 * xh + xl
    sib = 1 - core
    sgn = 1 - 2 * core
    home = core == xl
    away = core != xl
    pdx = 1 - 2 * xl

    def at(dx=0, dy=0, dz=0, to=None):
        nx, ny, nz = lax.rem(x + dx + 4, 4), lax.rem(y + dy + 4, 4), lax.rem(z + dz + 16, 16)
        to = core if to is None else to
        return (nz * 2 + lax.rem(nx, 2), (lax.div(nx, 2) * 4 + ny) * 2 + to)

    def remote(src, dst, send, recv, dev):
        pltpu.make_async_remote_copy(
            src_ref=src, dst_ref=dst, send_sem=send, recv_sem=recv, device_id=dev, device_id_type=MESH
        ).start()

    def wait(ref, sem):
        pltpu.make_async_copy(ref, ref, sem).wait()

    barrier = pltpu.get_barrier_semaphore()
    greet = [at(to=sib), at(dx=1), at(dx=-1), at(dx=pdx, to=sib), at(dy=1), at(dy=-1)]
    for dev in greet:
        pl.semaphore_signal(barrier, inc=1, device_id=dev, device_id_type=MESH)

    @pl.loop(1, 16)
    def _(d):
        pl.semaphore_signal(barrier, inc=1, device_id=at(dz=d), device_id_type=MESH)

    pl.semaphore_wait(barrier, len(greet) + 15)

    def rows(half):
        return pl.ds(half * 256, 256)

    def shard(kind, dx, dy):
        xs, ys = lax.rem(x + 4 - dx, 4), lax.rem(y + 4 - dy, 4)
        return (lax.div(xs, 2) * 4 + ys) * 2 + (core if kind == "A" else sib)

    def acts_event(event):
        kind, dx, dy, half = event
        k = shard(kind, dx, dy)
        here = X.at[k, rows(half)]
        if (kind, dx, dy) == ("A", 0, 0):
            src = acts.at[rows(half)]
        else:
            wait(here, rx.at[k, half])
            src = here
        for way in onward(*event):
            ddx, ddy = STEPS[way]
            remote(src, here, sx.at[k, half, way], rx.at[k, half], at(dx=ddx, dy=ddy))

    def acts_sent(event):
        kind, dx, dy, half = event
        k = shard(kind, dx, dy)
        for way in onward(*event):
            wait(X.at[k, rows(half)], sx.at[k, half, way])

    def piece(kind, zz, j):
        j128 = pl.multiple_of(j * 128, 128)
        if kind == 0:
            return WKV.at[zz, pl.ds(j128, 128), :]
        if kind == 1:
            return WQ.at[zz, pl.ds(j128, 128), :]
        return WO.at[zz, :, pl.ds(j128, 128)]

    def kv_part(j, i):
        return WKV.at[z, pl.ds(pl.multiple_of(j * 128, 128), 128), pl.ds(pl.multiple_of(i * 128, 128), 128)]

    def zrow(d):
        return lax.rem(z - sgn * d + 32, 16)

    def local_copies():
        yield wkv, kv_part(xl, core), loc.at[0], None
        yield wq, piece(1, z, xl), loc.at[1], home
        yield wo, piece(2, z, xl), loc.at[2], home
        yield acts, X.at[zero], loc.at[3], home

    def when(cond, f):
        if cond is None:
            f()
        else:
            pl.when(cond)(f)

    for src, dst, sem, cond in local_copies():
        when(cond, lambda: pltpu.make_async_copy(src, dst, sem).start())

    @pl.when(away)
    def _():
        for half in (0, 1):
            remote(acts.at[rows(half)], X.at[zero, rows(half)], sd.at[half], rx.at[zero, half], at(to=sib))

    remote(wkv, kv_part(xl, core), s0.at[0], r0kv.at[xl, core], at(to=sib))
    remote(wkv, kv_part(xl, core), s0.at[1], r0kv.at[xl, core], at(dx=pdx))
    remote(wkv, kv_part(xl, core), s0.at[2], r0kv.at[xl, core], at(dx=pdx, to=sib))

    def share(src, kind, sem, slot):
        @pl.when(home)
        def _():
            remote(src, piece(kind, z, xl), s0.at[slot], sem.at[xl], at(to=sib))

        @pl.when(away)
        def _():
            remote(src, piece(kind, z, xl), s0.at[slot], sem.at[xl], at(dx=pdx))
            remote(src, piece(kind, z, xl), s0.at[slot + 1], sem.at[xl], at(dx=pdx, to=sib))

    remote(tmask, TMR, sm.at[0], rm.at[0], at(dx=pdx))
    remote(amask, AMR, sm.at[1], rm.at[1], at(dx=pdx))

    def z_own(kind):
        for j in (xl, 1 - xl):
            own = j is xl
            if kind == 0:
                if own:
                    pltpu.make_async_copy(wkv, kv_part(xl, core), loc.at[0]).wait()
                    wait(kv_part(xl, sib), r0kv.at[xl, sib])
                else:
                    wait(kv_part(j, 0), r0kv.at[j, 0])
                    wait(kv_part(j, 1), r0kv.at[j, 1])
            else:
                src, sem = ((wq, r0q), (wo, r0o))[kind - 1]
                if own:
                    pl.when(home)(lambda: pltpu.make_async_copy(src, piece(kind, z, xl), loc.at[kind]).wait())
                    pl.when(away)(lambda: wait(piece(kind, z, xl), sem.at[xl]))
                else:
                    wait(piece(kind, z, j), sem.at[j])
            remote(piece(kind, z, j), piece(kind, z, j), sz.at[kind, 0, j], rz.at[kind, 0, j], at(dz=sgn))

    def z_step(kind, d):
        zz = zrow(d)
        for j in (0, 1) if d < 8 else (core,):
            ref = piece(kind, zz, j)
            wait(ref, rz.at[kind, d - 1, j])
            if d < 7:
                remote(ref, ref, sz.at[kind, d, j], rz.at[kind, d, j], at(dz=sgn))
            remote(ref, ref, ss.at[kind, d - 1, j], rs.at[kind, d - 1, j], at(to=sib))
        if d == 7:
            ref = piece(kind, zz, core)
            remote(ref, ref, sz.at[kind, d, core], rz.at[kind, d, core], at(dz=sgn))

    def z_sent(kind):
        for d in range(8):
            for j in (0, 1) if d < 7 else (core,):
                wait(piece(kind, z, j), sz.at[kind, d, j])
        for d in range(1, 9):
            for j in (0, 1) if d < 8 else (core,):
                wait(piece(kind, z, j), ss.at[kind, d - 1, j])

    def z_sib(kind, d):
        for j in (0, 1) if d < 8 else (sib,):
            wait(piece(kind, zrow(-d), j), rs.at[kind, d - 1, j])

    def acts_events(lo, hi):
        @pl.when(home)
        def _():
            for event in ORDER_HOME[lo:hi]:
                acts_event(event)

        @pl.when(away)
        def _():
            for event in ORDER_AWAY[lo:hi]:
                acts_event(event)

    pl.when(home)(lambda: [acts_event(e) for e in ORDER_HOME[:2]] and None)
    share(wq, 1, r0q, 3)
    z_own(0)
    z_own(1)
    pl.when(home)(lambda: [acts_event(e) for e in ORDER_HOME[2:8]] and None)
    pl.when(away)(lambda: [acts_event(e) for e in ORDER_AWAY[:6]] and None)
    share(wo, 2, r0o, 5)
    cuts_home = [8, 13, 17, 20, 24, 28, 32]
    cuts_away = [6, 11, 16, 22, 25, 28, 32]
    for d in range(1, 7):
        z_step(0, d)
        z_step(1, d)
        lo, hi = cuts_home[d - 1], cuts_home[d]
        pl.when(home)(lambda: [acts_event(e) for e in ORDER_HOME[lo:hi]] and None)
        lo, hi = cuts_away[d - 1], cuts_away[d]
        pl.when(away)(lambda: [acts_event(e) for e in ORDER_AWAY[lo:hi]] and None)
    for d in (7, 8):
        z_step(0, d)
        z_step(1, d)
    z_own(2)
    pl.when(home)(lambda: pltpu.make_async_copy(acts, X.at[zero], loc.at[3]).wait())
    for d in range(1, 9):
        z_sib(0, d)
        z_sib(1, d)

    ACCQ[...] = jnp.zeros_like(ACCQ)
    ACCK[...] = jnp.zeros_like(ACCK)
    SSQ[...] = jnp.zeros_like(SSQ)

    @pl.loop(0, 16)
    def _(k):
        v = X[k].astype(F32)
        sq = v * v
        SSQ[...] += sq[:, :128] + sq[:, 128:]
        g = gain[:, pl.ds(pl.multiple_of(k * 256, 256), 256)].astype(F32)
        scaled = (v * g).astype(BF16)
        ACCQ[...] += jnp.dot(scaled, WQ[k], preferred_element_type=F32)
        ACCK[...] += jnp.dot(scaled, WKV[k], preferred_element_type=F32)

    inv = lax.rsqrt(jnp.sum(SSQ[...], -1, keepdims=True) * (1.0 / 4096) + 1e-5)
    block = 2 * z + core
    cb, sb = coff[pl.ds(block, 1), :], soff[pl.ds(block, 1), :]
    lane = lax.broadcasted_iota(jnp.int32, (1, 128), 1)
    cos = cb * ctab[...] - sb * stab[...]
    sin = sb * ctab[...] + cb * stab[...]
    sin = jnp.where(lane < 64, -sin, sin)

    def rope(v):
        return v * cos + pltpu.roll(v, 64, 1) * sin

    KV[:, :128] = rope(ACCK[:, :128] * inv).astype(BF16)
    KV[:, 128:] = (ACCK[:, 128:] * inv).astype(BF16)

    anchor = aidx[0]
    anchor_z, anchor_core = lax.div(anchor, 2), lax.rem(anchor, 2)
    mine = pl.ds(pl.multiple_of(core * 256, 256), 256)
    remote(KV.at[pl.ds(pl.multiple_of(sib * 256, 256), 256)], AB, sa, ra, at(to=sib))
    for h in (0, 1):
        q = (rope(ACCQ[:, h * 128:(h + 1) * 128] * inv) * (128 ** -0.5)).astype(BF16)
        for i in range(4):
            QB[i, h * 128:(h + 1) * 128, :] = q[i * 128:(i + 1) * 128]
    wait(AB, ra)
    CAND[...] = jnp.where(anchor_core == core, KV[mine, :], AB[...]).reshape(16, 16, 256)

    @pl.loop(1, 16)
    def _(s):
        d = lax.rem(s + 7, 15) + 1
        to = lax.rem(z + d, 16)
        remote(CAND.at[to], AR.at[z], sar.at[d], rar.at[z], at(dz=d))

    AR[z] = CAND[z]

    for ref, got, dst in ((tmask, TMR, BOWN), (amask, AMR, BFAR)):
        wait(got, rm.at[0 if ref is tmask else 1])
        seen = jnp.where(home, ref[0], got[0])
        if ref is amask:
            seen = jnp.where(block != anchor, seen, 0)
        term = jnp.where(seen == 1, 0.0, MASKED).astype(F32)
        for i in range(4):
            for j in range(4):
                dst[i, :, j * 128:(j + 1) * 128] = jnp.broadcast_to(term[i:i + 1, j:j + 1], (8, 128))

    over = (((1,), (1,)), ((), ()))
    row = lax.rem(lax.broadcasted_iota(jnp.int32, (256, 128), 0), 128)
    col = lax.broadcasted_iota(jnp.int32, (256, 128), 1)
    causal = jnp.where(col <= row, 0.0, MASKED).astype(F32)
    for i in range(4):
        n = (i + 1) * 128
        s = lax.dot_general(QB[i], KV[:n, :128], over, preferred_element_type=F32) + BOWN[i, 0:1, :n]
        last = s[:, n - 128:] + causal
        s = last if i == 0 else jnp.concatenate([s[:, :n - 128], last], 1)
        m = jnp.max(s, -1, keepdims=True)
        p = jnp.exp(s - m)
        MS[i] = jnp.broadcast_to(m, (256, 128))
        LS[i] = jnp.broadcast_to(jnp.sum(p, -1, keepdims=True), (256, 128))
        ACC[i] = jnp.dot(p.astype(BF16), KV[:n, 128:], preferred_element_type=F32)

    z_step(2, 1)
    z_step(2, 2)
    z_step(2, 3)

    @pl.loop(1, 16)
    def _(d):
        frm = lax.rem(z + d, 16)
        wait(AR.at[frm], rar.at[frm])

    SEL[...] = AR[anchor_z]

    @pl.loop(1, 16)
    def _(s):
        d = lax.rem(s + 7, 15) + 1
        remote(SEL, AKV.at[core, z], sak.at[d], rak.at[z], at(dz=d))

    AKV[core, z] = SEL[...]
    z_step(2, 4)
    z_step(2, 5)
    z_step(2, 6)

    @pl.loop(1, 16)
    def _(d):
        frm = lax.rem(z + d, 16)
        wait(AKV.at[core, frm], rak.at[frm])

    remote(AKV.at[core], AKV.at[core], sad, rad, at(to=sib))
    z_step(2, 7)
    z_step(2, 8)
    wait(AKV.at[sib], rad)
    far = AKV[...].reshape(512, 256)
    for i in range(4):
        s = lax.dot_general(QB[i], far[:, :128], over, preferred_element_type=F32) + BFAR[i, 0:1, :]
        m0 = MS[i][:, :1]
        m = jnp.maximum(m0, jnp.max(s, -1, keepdims=True))
        p = jnp.exp(s - m)
        alpha = jnp.exp(m0 - m)
        total = LS[i][:, :1] * alpha + jnp.sum(p, -1, keepdims=True)
        o = ACC[i] * alpha + jnp.dot(p.astype(BF16), far[:, 128:], preferred_element_type=F32)
        o = (o / total).astype(BF16)
        for h in (0, 1):
            ATT[i * 128:(i + 1) * 128, h * 128:(h + 1) * 128] = o[h * 128:(h + 1) * 128]

    offsets = [0]
    for d in range(1, 8):
        offsets += [d, -d]
    offsets += [8]

    def block_of(u, half):
        return lax.rem(z + offsets[2 * u + half] + 32, 16)

    y1, y2, y3 = lax.rem(y + 1, 4), lax.rem(y + 2, 4), lax.rem(y + 3, 4)
    hr = lax.div(lax.rem(x + 1, 4), 2)
    hl = lax.div(lax.rem(x + 3, 4), 2)

    class Unit:
        def __init__(self, u):
            self.u = u
            self.xfirst = u % 2 == 0

        def xs(self, half, h):
            return PB.at[self.u, half, h] if self.xfirst else PB.at[self.u, half, h, y]

        def rxs(self, way, half):
            return RX.at[self.u, way, half] if self.xfirst else RX.at[self.u, way, half, 0]

        def ys(self, half, yy):
            return PB.at[self.u, half, xh, yy] if self.xfirst else PB.at[self.u, half, :, yy]

        def ryc(self, way):
            return RYC.at[self.u, way, 0] if self.xfirst else RYC.at[self.u, way]

        def ryf(self, way, half):
            return RYF.at[self.u, way, half, 0] if self.xfirst else RYF.at[self.u, way, half]

        def sendx(self, src, slot, dx, way, half):
            remote(src, self.rxs(way, half), spx.at[self.u, slot], rpx.at[self.u, way, half], at(dx=dx))

        def sendyc(self, src, slot, dy, way):
            remote(src, self.ryc(way), spy.at[self.u, slot], rpyc.at[self.u, way], at(dy=dy))

        def sendyf(self, src, slot, dy, way, half):
            remote(src, self.ryf(way, half), spy.at[self.u, slot], rpyf.at[self.u, way, half], at(dy=dy))

        def project(self):
            for half in (0, 1):
                b = block_of(self.u, half)
                part = jnp.dot(ATT[...], WO[b], preferred_element_type=F32).astype(BF16)
                PB[self.u, half] = part.reshape(2, 4, 64, 256)

        def x_begin(self):
            @pl.when(home)
            def _():
                self.sendx(self.xs(0, 1 - xh), 0, 1, 0, 0)
                self.sendx(self.xs(1, 1 - xh), 1, -1, 1, 1)

            @pl.when(away)
            def _():
                self.sendx(self.xs(1, hr), 0, 1, 0, 1)
                self.sendx(self.xs(0, hl), 1, -1, 1, 0)

        def add(self, ref, got):
            ref[...] = (ref[...].astype(F32) + got[...].astype(F32)).astype(BF16)

        def x_mid(self):
            @pl.when(away)
            def _():
                wait(self.rxs(0, 0), rpx.at[self.u, 0, 0])
                self.add(self.xs(0, hr), self.rxs(0, 0))
                self.sendx(self.xs(0, hr), 2, 1, 0, 0)
                wait(self.rxs(1, 1), rpx.at[self.u, 1, 1])
                self.add(self.xs(1, hl), self.rxs(1, 1))
                self.sendx(self.xs(1, hl), 3, -1, 1, 1)

        def total(self, ref, one, two):
            return ref[...].astype(F32) + one[...].astype(F32) + two[...].astype(F32)

        def finish(self, half, value):
            value = value.astype(BF16)
            low, high = value[:32], value[32:]
            b = pl.multiple_of(block_of(self.u, half) * 256, 256)
            out[:, pl.ds(b, 256)] = jnp.where(core == 0, low, high)
            SB[self.u, half] = jnp.where(core == 0, high, low)
            if half == 1:
                remote(SB.at[self.u], OB.at[self.u], spd.at[self.u], rpd.at[self.u], at(to=sib))

        def x_end(self):
            @pl.when(home)
            def _():
                for half in (0, 1):
                    for way in (0, 1):
                        wait(self.rxs(way, half), rpx.at[self.u, way, half])
                    value = self.total(self.xs(half, xh), self.rxs(0, half), self.rxs(1, half))
                    if self.xfirst:
                        self.xs(half, xh)[...] = value.astype(BF16)
                    else:
                        self.finish(half, value)

        def on_y(self, f):
            if self.xfirst:
                pl.when(home)(f)
            else:
                f()

        def y_begin(self):
            def f():
                self.sendyc(self.ys(0, y2), 0, 1, 0)
                self.sendyc(self.ys(1, y2), 1, -1, 1)
                self.sendyf(self.ys(1, y1), 2, 1, 0, 1)
                self.sendyf(self.ys(0, y3), 3, -1, 1, 0)

            self.on_y(f)

        def y_mid(self):
            def f():
                wait(self.ryc(0), rpyc.at[self.u, 0])
                self.add(self.ys(0, y1), self.ryc(0))
                self.sendyf(self.ys(0, y1), 4, 1, 0, 0)
                wait(self.ryc(1), rpyc.at[self.u, 1])
                self.add(self.ys(1, y3), self.ryc(1))
                self.sendyf(self.ys(1, y3), 5, -1, 1, 1)

            self.on_y(f)

        def y_end(self):
            def f():
                for half in (0, 1):
                    for way in (0, 1):
                        wait(self.ryf(way, half), rpyf.at[self.u, way, half])
                    value = self.total(self.ys(half, y), self.ryf(0, half), self.ryf(1, half))
                    if self.xfirst:
                        self.finish(half, value)
                    else:
                        self.ys(half, y)[...] = value.astype(BF16)

            self.on_y(f)

        def stage(self, s):
            if s == 0:
                self.project()
            if self.xfirst:
                parts = [[self.x_begin], [self.x_mid], [self.x_end, self.y_begin], [self.y_mid], [self.y_end]]
            else:
                parts = [[self.y_begin], [self.y_mid], [self.y_end, self.x_begin], [self.x_mid], [self.x_end]]
            for part in parts[s]:
                part()

        def sent(self):
            @pl.when(home)
            def _():
                for slot in (0, 1):
                    wait(self.rxs(0, 0), spx.at[self.u, slot])
                wait(SB.at[self.u], spd.at[self.u])

            @pl.when(away)
            def _():
                for slot in range(4):
                    wait(self.rxs(0, 0), spx.at[self.u, slot])

            def f():
                for slot in range(6):
                    wait(self.ryc(0), spy.at[self.u, slot])

            self.on_y(f)

        def collect(self):
            @pl.when(away)
            def _():
                wait(OB.at[self.u], rpd.at[self.u])
                for half in (0, 1):
                    b = pl.multiple_of(block_of(self.u, half) * 256, 256)
                    out[:, pl.ds(b, 256)] = OB[self.u, half]

    for d in range(1, 9):
        z_sib(2, d)
    units = [Unit(u) for u in range(UNITS)]
    for t in range(UNITS + 4 * LAG):
        for s in reversed(range(5)):
            u = t - s * LAG
            if 0 <= u < UNITS:
                units[u].stage(s)

    pl.when(home)(lambda: [acts_sent(e) for e in ORDER_HOME] and None)
    pl.when(away)(lambda: [acts_sent(e) for e in ORDER_AWAY] and None)

    @pl.when(away)
    def _():
        for half in (0, 1):
            wait(X.at[0, rows(half)], sd.at[half])

    for slot in range(3):
        wait(kv_part(0, 0), s0.at[slot])
    for slot, kind in ((3, 1), (5, 2)):
        wait(piece(kind, z, 0), s0.at[slot])

        @pl.when(away)
        def _():
            wait(piece(kind, z, 0), s0.at[slot + 1])

    wait(TMR, sm.at[0])
    wait(AMR, sm.at[1])
    for kind in range(3):
        z_sent(kind)
    wait(AB, sa)

    @pl.loop(1, 16)
    def _(d):
        wait(SEL, sar.at[d])
        wait(SEL, sak.at[d])

    wait(AKV.at[0], sad)
    for unit in units:
        unit.sent()
    for unit in units:
        unit.collect()


def tables():
    f = 500000.0 ** (-np.arange(64, dtype=np.float64) * 2.0 / 128)
    f = np.concatenate([f, f])
    inner = np.arange(512, dtype=np.float64)[:, None] * f
    outer = 512.0 * np.arange(32, dtype=np.float64)[:, None] * f
    return [t.astype(np.float32) for t in (np.cos(inner), np.sin(inner), np.cos(outer), np.sin(outer))]


def local(activations, norm_gain, query_weight, kv_weight, out_weight, tile_mask, anchor_mask, anchor_index):
    vmem = pl.BlockSpec(memory_space=pltpu.VMEM)
    smem = pl.BlockSpec(memory_space=pltpu.SMEM)
    V = pltpu.VMEM
    D = pltpu.SemaphoreType.DMA
    scratch = [
        V((16, 512, 256), BF16), V((16, 256, 256), BF16), V((16, 256, 256), BF16), V((16, 256, 256), BF16),
        V((512, 256), F32), V((512, 256), F32), V((512, 128), F32),
        V((4, 256, 128), BF16), V((512, 256), BF16),
        V((1, 4, 4), jnp.int32), V((1, 4, 4), jnp.int32), V((4, 8, 512), F32), V((4, 8, 512), F32),
        V((256, 256), BF16), V((16, 16, 256), BF16), V((16, 16, 256), BF16), V((16, 256), BF16),
        V((2, 16, 16, 256), BF16), V((4, 256, 128), F32), V((4, 256, 128), F32), V((4, 256, 128), F32),
        V((512, 256), BF16),
        V((UNITS, 2, 2, 4, 64, 256), BF16), V((UNITS, 2, 2, 4, 64, 256), BF16),
        V((UNITS, 2, 2, 64, 256), BF16), V((UNITS, 2, 2, 2, 64, 256), BF16),
        V((UNITS, 2, 32, 256), BF16), V((UNITS, 2, 32, 256), BF16),
        D((16, 2)), D((16, 2, 4)), D((2,)), D((4,)), D((2, 2)), D((2,)), D((2,)), D((7,)),
        D((3, 8, 2)), D((3, 8, 2)), D((3, 8, 2)), D((3, 8, 2)), D((2,)), D((2,)),
        D(()), D(()), D((16,)), D((16,)), D((16,)), D((16,)), D(()), D(()),
        D((UNITS, 2, 2)), D((UNITS, 4)), D((UNITS, 2)), D((UNITS, 2, 2)), D((UNITS, 6)), D((UNITS,)), D((UNITS,)),
    ]
    return pl.pallas_call(
        body,
        out_shape=jax.ShapeDtypeStruct((32, 4096), BF16),
        in_specs=[vmem] * 7 + [smem] + [vmem] * 4,
        out_specs=vmem,
        scratch_shapes=scratch,
        compiler_params=pltpu.CompilerParams(
            collective_id=0, has_side_effects=True, vmem_limit_bytes=60 * 1024 * 1024
        ),
        name="star",
    )(
        activations, norm_gain.reshape(1, 4096), query_weight, kv_weight[:, 0, :], out_weight,
        tile_mask, anchor_mask, anchor_index, *[jnp.asarray(t) for t in tables()],
    )


def solution(mesh):
    placed = (
        P("ctx", "zero"), P(), P("ctx", "zero"), P("ctx", "zero", None), P("zero", "ctx"),
        P("ctx", None, None), P("ctx", None, None), P(),
    )
    return jax.shard_map(
        local, mesh=mesh, in_specs=placed, out_specs=P(("ctx", "zero"), None), check_vma=False
    )
```

```python
import functools

import numpy as np

import jax
import jax.numpy as jnp
from jax import lax
from jax.experimental import pallas as pl
from jax.experimental.pallas import tpu as pltpu
from jax.sharding import PartitionSpec as P

MESH = pl.DeviceIdType.MESH
F32 = jnp.float32
BF16 = jnp.bfloat16
MASKED = -1e30
UNITS = 8
LAG = 3

ORDER_HOME = [
    ("A", 0, 0, 0), ("A", 0, 0, 1), ("B", 0, 0, 0), ("B", 0, 0, 1), ("A", 0, 3, 0), ("A", 0, 1, 0),
    ("A", 0, 3, 1), ("A", 0, 1, 1), ("B", 0, 3, 0), ("B", 0, 1, 0), ("B", 0, 3, 1), ("B", 0, 1, 1),
    ("A", 0, 2, 0), ("A", 2, 0, 0), ("A", 2, 0, 1), ("B", 2, 0, 0), ("A", 0, 2, 1), ("B", 0, 2, 0),
    ("B", 0, 2, 1), ("B", 2, 0, 1), ("A", 2, 3, 0), ("A", 2, 1, 0), ("B", 2, 3, 0), ("B", 2, 3, 1),
    ("A", 2, 3, 1), ("A", 2, 1, 1), ("B", 2, 1, 0), ("B", 2, 1, 1), ("A", 2, 2, 0), ("A", 2, 2, 1),
    ("B", 2, 2, 0), ("B", 2, 2, 1),
]
ORDER_AWAY = [
    ("A", 1, 0, 0), ("A", 3, 0, 0), ("A", 1, 0, 1), ("A", 3, 0, 1), ("B", 1, 0, 0), ("B", 3, 0, 0),
    ("B", 1, 0, 1), ("B", 3, 0, 1), ("A", 1, 3, 0), ("A", 1, 1, 0), ("A", 3, 3, 0), ("B", 1, 3, 0),
    ("B", 3, 3, 0), ("A", 3, 1, 0), ("A", 1, 3, 1), ("B", 1, 1, 0), ("B", 3, 1, 0), ("A", 1, 1, 1),
    ("B", 3, 3, 1), ("A", 3, 3, 1), ("A", 3, 1, 1), ("B", 1, 3, 1), ("B", 3, 1, 1), ("B", 1, 1, 1),
    ("A", 1, 2, 0), ("B", 3, 2, 0), ("A", 1, 2, 1), ("B", 1, 2, 0), ("B", 3, 2, 1), ("A", 3, 2, 0),
    ("A", 3, 2, 1), ("B", 1, 2, 1),
]
STEPS = [(1, 0), (-1, 0), (0, 1), (0, -1)]
XP, XM, YP, YM = range(4)


def onward(kind, dx, dy, half):
    first, second = (dx, dy) if kind == "A" else (dy, dx)
    fp, fm, sp, sm = (XP, XM, YP, YM) if kind == "A" else (YP, YM, XP, XM)
    ways = []
    if second == 0:
        if first == 0:
            ways += [fp, fm]
        if first == 1 and half == 0:
            ways += [fp]
        if first == 3 and half == 1:
            ways += [fm]
        ways += [sp, sm]
    if second == 1 and half == 0:
        ways += [sp]
    if second == 3 and half == 1:
        ways += [sm]
    return ways


def body(
    acts, gain, wq, wkv, wo, tmask, amask, aidx, ctab, stab, coff, soff, out,
    GAIN, CT, ST, CO, SO, AIDX, TM, AM,
    X, WQ, WKV, WO, ACCQ, ACCK, SSQ, QB, KV, TMR, AMR, BOWN, BFAR,
    AB, CAND, AR, SEL, AKV, MS, LS, ACC, ATT, PB, RX, RYC, RYF, SB, OB,
    ld, rx, sx, sd, loc, r0kv, r0q, r0o, s0, rz, sz, rs, ss, rm, sm,
    ra, sa, rar, sar, rak, sak, rad, sad,
    rpx, spx, rpyc, rpyf, spy, rpd, spd,
):
    ctx = lax.axis_index("ctx")
    zero = lax.axis_index("zero")
    z, xl = lax.div(ctx, 2), lax.rem(ctx, 2)
    xh, y, core = lax.div(zero, 8), lax.rem(lax.div(zero, 2), 4), lax.rem(zero, 2)
    x = 2 * xh + xl
    sib = 1 - core
    sgn = 1 - 2 * core
    home = core == xl
    away = core != xl
    pdx = 1 - 2 * xl

    def at(dx=0, dy=0, dz=0, to=None):
        nx, ny, nz = lax.rem(x + dx + 4, 4), lax.rem(y + dy + 4, 4), lax.rem(z + dz + 16, 16)
        to = core if to is None else to
        return (nz * 2 + lax.rem(nx, 2), (lax.div(nx, 2) * 4 + ny) * 2 + to)

    def remote(src, dst, send, recv, dev):
        pltpu.make_async_remote_copy(
            src_ref=src, dst_ref=dst, send_sem=send, recv_sem=recv, device_id=dev, device_id_type=MESH
        ).start()

    def wait(ref, sem):
        pltpu.make_async_copy(ref, ref, sem).wait()

    barrier = pltpu.get_barrier_semaphore()
    greet = [at(to=sib), at(dx=1), at(dx=-1), at(dx=pdx, to=sib), at(dy=1), at(dy=-1), at(dz=1), at(dz=-1)]
    for dev in greet:
        pl.semaphore_signal(barrier, inc=1, device_id=dev, device_id_type=MESH)

    loads = [
        pltpu.make_async_copy(src, dst, ld.at[n])
        for n, (src, dst) in enumerate(
            [(gain, GAIN), (ctab, CT), (stab, ST), (coff, CO), (soff, SO), (aidx, AIDX), (tmask, TM), (amask, AM)]
        )
    ]
    for copy in loads:
        copy.start()
    pl.semaphore_wait(barrier, len(greet))

    def rows(half):
        return pl.ds(half * 256, 256)

    def shard(kind, dx, dy):
        xs, ys = lax.rem(x + 4 - dx, 4), lax.rem(y + 4 - dy, 4)
        return (lax.div(xs, 2) * 4 + ys) * 2 + (core if kind == "A" else sib)

    def acts_event(event):
        kind, dx, dy, half = event
        k = shard(kind, dx, dy)
        here = X.at[k, rows(half)]
        if (kind, dx, dy) == ("A", 0, 0):
            src = acts.at[rows(half)]
        else:
            wait(here, rx.at[k, half])
            src = here
        for way in onward(*event):
            ddx, ddy = STEPS[way]
            remote(src, here, sx.at[k, half, way], rx.at[k, half], at(dx=ddx, dy=ddy))

    def acts_sent(event):
        kind, dx, dy, half = event
        k = shard(kind, dx, dy)
        for way in onward(*event):
            wait(X.at[k, rows(half)], sx.at[k, half, way])

    def piece(kind, zz, j):
        j128 = pl.multiple_of(j * 128, 128)
        if kind == 0:
            return WKV.at[zz, pl.ds(j128, 128), :]
        if kind == 1:
            return WQ.at[zz, pl.ds(j128, 128), :]
        return WO.at[zz, j]

    def kv_part(j, i):
        return WKV.at[z, pl.ds(pl.multiple_of(j * 128, 128), 128), pl.ds(pl.multiple_of(i * 128, 128), 128)]

    def zrow(d):
        return lax.rem(z - sgn * d + 32, 16)

    def local_copies():
        yield wkv, kv_part(xl, core), loc.at[0], None
        yield wq, piece(1, z, xl), loc.at[1], home
        yield wo, piece(2, z, xl), loc.at[2], home
        yield acts, X.at[zero], loc.at[3], home

    def when(cond, f):
        if cond is None:
            f()
        else:
            pl.when(cond)(f)

    for src, dst, sem, cond in local_copies():
        when(cond, lambda: pltpu.make_async_copy(src, dst, sem).start())

    @pl.when(away)
    def _():
        for half in (0, 1):
            remote(acts.at[rows(half)], X.at[zero, rows(half)], sd.at[half], rx.at[zero, half], at(to=sib))

    remote(wkv, kv_part(xl, core), s0.at[0], r0kv.at[xl, core], at(to=sib))
    remote(wkv, kv_part(xl, core), s0.at[1], r0kv.at[xl, core], at(dx=pdx))
    remote(wkv, kv_part(xl, core), s0.at[2], r0kv.at[xl, core], at(dx=pdx, to=sib))

    def share(src, kind, sem, slot):
        @pl.when(home)
        def _():
            remote(src, piece(kind, z, xl), s0.at[slot], sem.at[xl], at(to=sib))

        @pl.when(away)
        def _():
            remote(src, piece(kind, z, xl), s0.at[slot], sem.at[xl], at(dx=pdx))
            remote(src, piece(kind, z, xl), s0.at[slot + 1], sem.at[xl], at(dx=pdx, to=sib))

    remote(tmask, TMR, sm.at[0], rm.at[0], at(dx=pdx))
    remote(amask, AMR, sm.at[1], rm.at[1], at(dx=pdx))

    def z_own(kind):
        for j in (xl, 1 - xl):
            own = j is xl
            if kind == 0:
                if own:
                    pltpu.make_async_copy(wkv, kv_part(xl, core), loc.at[0]).wait()
                    wait(kv_part(xl, sib), r0kv.at[xl, sib])
                else:
                    wait(kv_part(j, 0), r0kv.at[j, 0])
                    wait(kv_part(j, 1), r0kv.at[j, 1])
            else:
                src, sem = ((wq, r0q), (wo, r0o))[kind - 1]
                if own:
                    pl.when(home)(lambda: pltpu.make_async_copy(src, piece(kind, z, xl), loc.at[kind]).wait())
                    pl.when(away)(lambda: wait(piece(kind, z, xl), sem.at[xl]))
                else:
                    wait(piece(kind, z, j), sem.at[j])
            remote(piece(kind, z, j), piece(kind, z, j), sz.at[kind, 0, j], rz.at[kind, 0, j], at(dz=sgn))

    def z_step(kind, d):
        zz = zrow(d)
        for j in (0, 1) if d < 8 else (core,):
            ref = piece(kind, zz, j)
            wait(ref, rz.at[kind, d - 1, j])
            if d < 7:
                remote(ref, ref, sz.at[kind, d, j], rz.at[kind, d, j], at(dz=sgn))
            remote(ref, ref, ss.at[kind, d - 1, j], rs.at[kind, d - 1, j], at(to=sib))
        if d == 7:
            ref = piece(kind, zz, core)
            remote(ref, ref, sz.at[kind, d, core], rz.at[kind, d, core], at(dz=sgn))

    def z_sent(kind):
        for d in range(8):
            for j in (0, 1) if d < 7 else (core,):
                wait(piece(kind, z, j), sz.at[kind, d, j])
        for d in range(1, 9):
            for j in (0, 1) if d < 8 else (core,):
                wait(piece(kind, z, j), ss.at[kind, d - 1, j])

    def z_sib(kind, d):
        for j in (0, 1) if d < 8 else (sib,):
            wait(piece(kind, zrow(-d), j), rs.at[kind, d - 1, j])

    def acts_events(lo, hi):
        @pl.when(home)
        def _():
            for event in ORDER_HOME[lo:hi]:
                acts_event(event)

        @pl.when(away)
        def _():
            for event in ORDER_AWAY[lo:hi]:
                acts_event(event)

    pl.when(home)(lambda: [acts_event(e) for e in ORDER_HOME[:2]] and None)
    share(wq, 1, r0q, 3)
    z_own(0)
    z_own(1)
    pl.when(home)(lambda: [acts_event(e) for e in ORDER_HOME[2:8]] and None)
    pl.when(away)(lambda: [acts_event(e) for e in ORDER_AWAY[:6]] and None)
    share(wo, 2, r0o, 5)
    cuts_home = [8, 13, 17, 20, 24, 28, 32]
    cuts_away = [6, 11, 16, 22, 25, 28, 32]
    for d in range(1, 7):
        z_step(0, d)
        z_step(1, d)
        if d == 2:
            z_own(2)
        if d > 2:
            z_step(2, d - 2)
        lo, hi = cuts_home[d - 1], cuts_home[d]
        pl.when(home)(lambda: [acts_event(e) for e in ORDER_HOME[lo:hi]] and None)
        lo, hi = cuts_away[d - 1], cuts_away[d]
        pl.when(away)(lambda: [acts_event(e) for e in ORDER_AWAY[lo:hi]] and None)
    for d in (7, 8):
        z_step(0, d)
        z_step(1, d)
        z_step(2, d - 2)
    pl.when(home)(lambda: pltpu.make_async_copy(acts, X.at[zero], loc.at[3]).wait())
    for d in range(1, 9):
        z_sib(0, d)
        z_sib(1, d)

    for copy in loads:
        copy.wait()
    ACCQ[...] = jnp.zeros_like(ACCQ)
    ACCK[...] = jnp.zeros_like(ACCK)
    SSQ[...] = jnp.zeros_like(SSQ)

    @pl.loop(0, 16)
    def _(k):
        v = X[k].astype(F32)
        sq = v * v
        SSQ[...] += sq[:, :128] + sq[:, 128:]
        g = GAIN[pl.ds(pl.multiple_of(k * 256, 256), 256)].astype(F32)[None, :]
        scaled = (v * g).astype(BF16)
        ACCQ[...] += jnp.dot(scaled, WQ[k], preferred_element_type=F32)
        ACCK[...] += jnp.dot(scaled, WKV[k], preferred_element_type=F32)

    inv = lax.rsqrt(jnp.sum(SSQ[...], -1, keepdims=True) * (1.0 / 4096) + 1e-5)
    block = 2 * z + core
    cb, sb = CO[pl.ds(block, 1), :], SO[pl.ds(block, 1), :]
    lane = lax.broadcasted_iota(jnp.int32, (1, 128), 1)
    cos = cb * CT[...] - sb * ST[...]
    sin = sb * CT[...] + cb * ST[...]
    sin = jnp.where(lane < 64, -sin, sin)

    def rope(v):
        return v * cos + pltpu.roll(v, 64, 1) * sin

    KV[:, :128] = rope(ACCK[:, :128] * inv).astype(BF16)
    KV[:, 128:] = (ACCK[:, 128:] * inv).astype(BF16)

    anchor = AIDX[0]
    anchor_z, anchor_core = lax.div(anchor, 2), lax.rem(anchor, 2)
    mine = pl.ds(pl.multiple_of(core * 256, 256), 256)
    remote(KV.at[pl.ds(pl.multiple_of(sib * 256, 256), 256)], AB, sa, ra, at(to=sib))
    for h in (0, 1):
        q = (rope(ACCQ[:, h * 128:(h + 1) * 128] * inv) * (128 ** -0.5)).astype(BF16)
        for i in range(4):
            QB[i, h * 128:(h + 1) * 128, :] = q[i * 128:(i + 1) * 128]
    wait(AB, ra)
    CAND[...] = jnp.where(anchor_core == core, KV[mine, :], AB[...]).reshape(16, 16, 256)

    @pl.loop(1, 16)
    def _(s):
        d = lax.rem(s + 7, 15) + 1
        to = lax.rem(z + d, 16)
        remote(CAND.at[to], AR.at[z], sar.at[d], rar.at[z], at(dz=d))

    AR[z] = CAND[z]

    for ref, got, dst in ((TM, TMR, BOWN), (AM, AMR, BFAR)):
        wait(got, rm.at[0 if ref is TM else 1])
        seen = jnp.where(home, ref[0], got[0])
        if ref is AM:
            seen = jnp.where(block != anchor, seen, 0)
        term = jnp.where(seen == 1, 0.0, MASKED).astype(F32)
        for i in range(4):
            for j in range(4):
                dst[i, :, j * 128:(j + 1) * 128] = jnp.broadcast_to(term[i:i + 1, j:j + 1], (8, 128))

    over = (((1,), (1,)), ((), ()))
    row = lax.rem(lax.broadcasted_iota(jnp.int32, (256, 128), 0), 128)
    col = lax.broadcasted_iota(jnp.int32, (256, 128), 1)
    causal = jnp.where(col <= row, 0.0, MASKED).astype(F32)
    for i in range(4):
        n = (i + 1) * 128
        s = lax.dot_general(QB[i], KV[:n, :128], over, preferred_element_type=F32) + BOWN[i, 0:1, :n]
        last = s[:, n - 128:] + causal
        s = last if i == 0 else jnp.concatenate([s[:, :n - 128], last], 1)
        m = jnp.max(s, -1, keepdims=True)
        p = jnp.exp(s - m)
        MS[i] = jnp.broadcast_to(m, (256, 128))
        LS[i] = jnp.broadcast_to(jnp.sum(p, -1, keepdims=True), (256, 128))
        ACC[i] = jnp.dot(p.astype(BF16), KV[:n, 128:], preferred_element_type=F32)

    z_step(2, 7)

    @pl.loop(1, 16)
    def _(d):
        frm = lax.rem(z + d, 16)
        wait(AR.at[frm], rar.at[frm])

    SEL[...] = AR[anchor_z]

    @pl.loop(1, 16)
    def _(s):
        d = lax.rem(s + 7, 15) + 1
        remote(SEL, AKV.at[core, z], sak.at[d], rak.at[z], at(dz=d))

    AKV[core, z] = SEL[...]
    z_step(2, 8)

    @pl.loop(1, 16)
    def _(d):
        frm = lax.rem(z + d, 16)
        wait(AKV.at[core, frm], rak.at[frm])

    remote(AKV.at[core], AKV.at[core], sad, rad, at(to=sib))
    wait(AKV.at[sib], rad)
    far = AKV[...].reshape(512, 256)
    for i in range(4):
        s = lax.dot_general(QB[i], far[:, :128], over, preferred_element_type=F32) + BFAR[i, 0:1, :]
        m0 = MS[i][:, :1]
        m = jnp.maximum(m0, jnp.max(s, -1, keepdims=True))
        p = jnp.exp(s - m)
        alpha = jnp.exp(m0 - m)
        total = LS[i][:, :1] * alpha + jnp.sum(p, -1, keepdims=True)
        o = ACC[i] * alpha + jnp.dot(p.astype(BF16), far[:, 128:], preferred_element_type=F32)
        o = (o / total).astype(BF16)
        for h in (0, 1):
            ATT[i * 128:(i + 1) * 128, h * 128:(h + 1) * 128] = o[h * 128:(h + 1) * 128]

    offsets = [0]
    for d in range(1, 8):
        offsets += [d, -d]
    offsets += [8]

    def block_of(u, half):
        return lax.rem(z + offsets[2 * u + half] + 32, 16)

    y1, y2, y3 = lax.rem(y + 1, 4), lax.rem(y + 2, 4), lax.rem(y + 3, 4)
    hr = lax.div(lax.rem(x + 1, 4), 2)
    hl = lax.div(lax.rem(x + 3, 4), 2)

    class Unit:
        def __init__(self, u):
            self.u = u
            self.xfirst = u % 2 == 0

        def xs(self, half, h):
            return PB.at[self.u, half, h] if self.xfirst else PB.at[self.u, half, h, y]

        def rxs(self, way, half):
            return RX.at[self.u, way, half] if self.xfirst else RX.at[self.u, way, half, 0]

        def ys(self, half, yy):
            return PB.at[self.u, half, xh, yy] if self.xfirst else PB.at[self.u, half, :, yy]

        def ryc(self, way):
            return RYC.at[self.u, way, 0] if self.xfirst else RYC.at[self.u, way]

        def ryf(self, way, half):
            return RYF.at[self.u, way, half, 0] if self.xfirst else RYF.at[self.u, way, half]

        def sendx(self, src, slot, dx, way, half):
            remote(src, self.rxs(way, half), spx.at[self.u, slot], rpx.at[self.u, way, half], at(dx=dx))

        def sendyc(self, src, slot, dy, way):
            remote(src, self.ryc(way), spy.at[self.u, slot], rpyc.at[self.u, way], at(dy=dy))

        def sendyf(self, src, slot, dy, way, half):
            remote(src, self.ryf(way, half), spy.at[self.u, slot], rpyf.at[self.u, way, half], at(dy=dy))

        def project(self):
            for half in (0, 1):
                b = block_of(self.u, half)
                w = jnp.concatenate([WO[b, 0], WO[b, 1]], 1)
                part = jnp.dot(ATT[...], w, preferred_element_type=F32).astype(BF16)
                PB[self.u, half] = part.reshape(2, 4, 64, 256)

        def x_begin(self):
            @pl.when(home)
            def _():
                self.sendx(self.xs(0, 1 - xh), 0, 1, 0, 0)
                self.sendx(self.xs(1, 1 - xh), 1, -1, 1, 1)

            @pl.when(away)
            def _():
                self.sendx(self.xs(1, hr), 0, 1, 0, 1)
                self.sendx(self.xs(0, hl), 1, -1, 1, 0)

        def add(self, ref, got):
            ref[...] = (ref[...].astype(F32) + got[...].astype(F32)).astype(BF16)

        def x_mid(self):
            @pl.when(away)
            def _():
                wait(self.rxs(0, 0), rpx.at[self.u, 0, 0])
                self.add(self.xs(0, hr), self.rxs(0, 0))
                self.sendx(self.xs(0, hr), 2, 1, 0, 0)
                wait(self.rxs(1, 1), rpx.at[self.u, 1, 1])
                self.add(self.xs(1, hl), self.rxs(1, 1))
                self.sendx(self.xs(1, hl), 3, -1, 1, 1)

        def total(self, ref, one, two):
            return ref[...].astype(F32) + one[...].astype(F32) + two[...].astype(F32)

        def finish(self, half, value):
            value = value.astype(BF16)
            low, high = value[:32], value[32:]
            b = pl.multiple_of(block_of(self.u, half) * 256, 256)
            out[:, pl.ds(b, 256)] = jnp.where(core == 0, low, high)
            SB[self.u, half] = jnp.where(core == 0, high, low)
            if half == 1:
                remote(SB.at[self.u], OB.at[self.u], spd.at[self.u], rpd.at[self.u], at(to=sib))

        def x_end(self):
            @pl.when(home)
            def _():
                for half in (0, 1):
                    for way in (0, 1):
                        wait(self.rxs(way, half), rpx.at[self.u, way, half])
                    value = self.total(self.xs(half, xh), self.rxs(0, half), self.rxs(1, half))
                    if self.xfirst:
                        self.xs(half, xh)[...] = value.astype(BF16)
                    else:
                        self.finish(half, value)

        def on_y(self, f):
            if self.xfirst:
                pl.when(home)(f)
            else:
                f()

        def y_begin(self):
            def f():
                self.sendyc(self.ys(0, y2), 0, 1, 0)
                self.sendyc(self.ys(1, y2), 1, -1, 1)
                self.sendyf(self.ys(1, y1), 2, 1, 0, 1)
                self.sendyf(self.ys(0, y3), 3, -1, 1, 0)

            self.on_y(f)

        def y_mid(self):
            def f():
                wait(self.ryc(0), rpyc.at[self.u, 0])
                self.add(self.ys(0, y1), self.ryc(0))
                self.sendyf(self.ys(0, y1), 4, 1, 0, 0)
                wait(self.ryc(1), rpyc.at[self.u, 1])
                self.add(self.ys(1, y3), self.ryc(1))
                self.sendyf(self.ys(1, y3), 5, -1, 1, 1)

            self.on_y(f)

        def y_end(self):
            def f():
                for half in (0, 1):
                    for way in (0, 1):
                        wait(self.ryf(way, half), rpyf.at[self.u, way, half])
                    value = self.total(self.ys(half, y), self.ryf(0, half), self.ryf(1, half))
                    if self.xfirst:
                        self.finish(half, value)
                    else:
                        self.ys(half, y)[...] = value.astype(BF16)

            self.on_y(f)

        def stage(self, s):
            if s == 0:
                self.project()
            if self.xfirst:
                parts = [[self.x_begin], [self.x_mid], [self.x_end, self.y_begin], [self.y_mid], [self.y_end]]
            else:
                parts = [[self.y_begin], [self.y_mid], [self.y_end, self.x_begin], [self.x_mid], [self.x_end]]
            for part in parts[s]:
                part()

        def sent(self):
            @pl.when(home)
            def _():
                for slot in (0, 1):
                    wait(self.rxs(0, 0), spx.at[self.u, slot])
                wait(SB.at[self.u], spd.at[self.u])

            @pl.when(away)
            def _():
                for slot in range(4):
                    wait(self.rxs(0, 0), spx.at[self.u, slot])

            def f():
                for slot in range(6):
                    wait(self.ryc(0), spy.at[self.u, slot])

            self.on_y(f)

        def collect(self):
            @pl.when(away)
            def _():
                wait(OB.at[self.u], rpd.at[self.u])
                for half in (0, 1):
                    b = pl.multiple_of(block_of(self.u, half) * 256, 256)
                    out[:, pl.ds(b, 256)] = OB[self.u, half]

    for d in range(1, 9):
        z_sib(2, d)
    units = [Unit(u) for u in range(UNITS)]
    for t in range(UNITS + 4 * LAG):
        for s in reversed(range(5)):
            u = t - s * LAG
            if 0 <= u < UNITS:
                units[u].stage(s)

    pl.when(home)(lambda: [acts_sent(e) for e in ORDER_HOME] and None)
    pl.when(away)(lambda: [acts_sent(e) for e in ORDER_AWAY] and None)

    @pl.when(away)
    def _():
        for half in (0, 1):
            wait(X.at[0, rows(half)], sd.at[half])

    for slot in range(3):
        wait(kv_part(0, 0), s0.at[slot])
    for slot, kind in ((3, 1), (5, 2)):
        wait(piece(kind, z, 0), s0.at[slot])

        @pl.when(away)
        def _():
            wait(piece(kind, z, 0), s0.at[slot + 1])

    wait(TMR, sm.at[0])
    wait(AMR, sm.at[1])
    for kind in range(3):
        z_sent(kind)
    wait(AB, sa)

    @pl.loop(1, 16)
    def _(d):
        wait(SEL, sar.at[d])
        wait(SEL, sak.at[d])

    wait(AKV.at[0], sad)
    for unit in units:
        unit.sent()
    for unit in units:
        unit.collect()


def tables():
    f = 500000.0 ** (-np.arange(64, dtype=np.float64) * 2.0 / 128)
    f = np.concatenate([f, f])
    inner = np.arange(512, dtype=np.float64)[:, None] * f
    outer = 512.0 * np.arange(32, dtype=np.float64)[:, None] * f
    return [t.astype(np.float32) for t in (np.cos(inner), np.sin(inner), np.cos(outer), np.sin(outer))]


def local(activations, norm_gain, query_weight, kv_weight, out_weight, tile_mask, anchor_mask, anchor_index):
    vmem = pl.BlockSpec(memory_space=pltpu.VMEM)
    V = pltpu.VMEM
    D = pltpu.SemaphoreType.DMA
    scratch = [
        V((4096,), BF16), V((512, 128), F32), V((512, 128), F32), V((32, 128), F32), V((32, 128), F32),
        pltpu.SMEM((1,), jnp.int32), V((1, 4, 4), jnp.int32), V((1, 4, 4), jnp.int32),
        V((16, 512, 256), BF16), V((16, 256, 256), BF16), V((16, 256, 256), BF16), V((16, 2, 256, 128), BF16),
        V((512, 256), F32), V((512, 256), F32), V((512, 128), F32),
        V((4, 256, 128), BF16), V((512, 256), BF16),
        V((1, 4, 4), jnp.int32), V((1, 4, 4), jnp.int32), V((4, 8, 512), F32), V((4, 8, 512), F32),
        V((256, 256), BF16), V((16, 16, 256), BF16), V((16, 16, 256), BF16), V((16, 256), BF16),
        V((2, 16, 16, 256), BF16), V((4, 256, 128), F32), V((4, 256, 128), F32), V((4, 256, 128), F32),
        V((512, 256), BF16),
        V((UNITS, 2, 2, 4, 64, 256), BF16), V((UNITS, 2, 2, 4, 64, 256), BF16),
        V((UNITS, 2, 2, 64, 256), BF16), V((UNITS, 2, 2, 2, 64, 256), BF16),
        V((UNITS, 2, 32, 256), BF16), V((UNITS, 2, 32, 256), BF16),
        D((8,)),
        D((16, 2)), D((16, 2, 4)), D((2,)), D((4,)), D((2, 2)), D((2,)), D((2,)), D((7,)),
        D((3, 8, 2)), D((3, 8, 2)), D((3, 8, 2)), D((3, 8, 2)), D((2,)), D((2,)),
        D(()), D(()), D((16,)), D((16,)), D((16,)), D((16,)), D(()), D(()),
        D((UNITS, 2, 2)), D((UNITS, 4)), D((UNITS, 2)), D((UNITS, 2, 2)), D((UNITS, 6)), D((UNITS,)), D((UNITS,)),
    ]
    return pl.pallas_call(
        body,
        out_shape=jax.ShapeDtypeStruct((32, 4096), BF16),
        in_specs=[pl.BlockSpec(memory_space=pl.ANY)] * 12,
        out_specs=vmem,
        scratch_shapes=scratch,
        compiler_params=pltpu.CompilerParams(
            collective_id=0, has_side_effects=True, vmem_limit_bytes=60 * 1024 * 1024
        ),
        name="star",
    )(
        activations, norm_gain, query_weight, kv_weight[:, 0, :], out_weight,
        tile_mask, anchor_mask, anchor_index, *[jnp.asarray(t) for t in tables()],
    )


def solution(mesh):
    placed = (
        P("ctx", "zero"), P(), P("ctx", "zero"), P("ctx", "zero", None), P("zero", "ctx"),
        P("ctx", None, None), P("ctx", None, None), P(),
    )
    return jax.shard_map(
        local, mesh=mesh, in_specs=placed, out_specs=P(("ctx", "zero"), None), check_vma=False
    )
```

```python
import functools

import numpy as np

import jax
import jax.numpy as jnp
from jax import lax
from jax.experimental import pallas as pl
from jax.experimental.pallas import tpu as pltpu
from jax.sharding import PartitionSpec as P

MESH = pl.DeviceIdType.MESH
F32 = jnp.float32
BF16 = jnp.bfloat16
MASKED = -1e30
UNITS = 8
LAG = 4

ORDER_HOME = [
    ("A", 0, 0, 0), ("A", 0, 0, 1), ("B", 0, 0, 0), ("B", 0, 0, 1), ("A", 0, 3, 0), ("A", 0, 1, 0),
    ("A", 0, 3, 1), ("A", 0, 1, 1), ("B", 0, 3, 0), ("B", 0, 1, 0), ("B", 0, 3, 1), ("B", 0, 1, 1),
    ("A", 0, 2, 0), ("A", 2, 0, 0), ("A", 2, 0, 1), ("B", 2, 0, 0), ("A", 0, 2, 1), ("B", 0, 2, 0),
    ("B", 0, 2, 1), ("B", 2, 0, 1), ("A", 2, 3, 0), ("A", 2, 1, 0), ("B", 2, 3, 0), ("B", 2, 3, 1),
    ("A", 2, 3, 1), ("A", 2, 1, 1), ("B", 2, 1, 0), ("B", 2, 1, 1), ("A", 2, 2, 0), ("A", 2, 2, 1),
    ("B", 2, 2, 0), ("B", 2, 2, 1),
]
ORDER_AWAY = [
    ("A", 1, 0, 0), ("A", 3, 0, 0), ("A", 1, 0, 1), ("A", 3, 0, 1), ("B", 1, 0, 0), ("B", 3, 0, 0),
    ("B", 1, 0, 1), ("B", 3, 0, 1), ("A", 1, 3, 0), ("A", 1, 1, 0), ("A", 3, 3, 0), ("B", 1, 3, 0),
    ("B", 3, 3, 0), ("A", 3, 1, 0), ("A", 1, 3, 1), ("B", 1, 1, 0), ("B", 3, 1, 0), ("A", 1, 1, 1),
    ("B", 3, 3, 1), ("A", 3, 3, 1), ("A", 3, 1, 1), ("B", 1, 3, 1), ("B", 3, 1, 1), ("B", 1, 1, 1),
    ("A", 1, 2, 0), ("B", 3, 2, 0), ("A", 1, 2, 1), ("B", 1, 2, 0), ("B", 3, 2, 1), ("A", 3, 2, 0),
    ("A", 3, 2, 1), ("B", 1, 2, 1),
]
STEPS = [(1, 0), (-1, 0), (0, 1), (0, -1)]
XP, XM, YP, YM = range(4)


def onward(kind, dx, dy, half):
    first, second = (dx, dy) if kind == "A" else (dy, dx)
    fp, fm, sp, sm = (XP, XM, YP, YM) if kind == "A" else (YP, YM, XP, XM)
    ways = []
    if second == 0:
        if first == 0:
            ways += [fp, fm]
        if first == 1 and half == 0:
            ways += [fp]
        if first == 3 and half == 1:
            ways += [fm]
        ways += [sp, sm]
    if second == 1 and half == 0:
        ways += [sp]
    if second == 3 and half == 1:
        ways += [sm]
    return ways


def body(
    acts, gain, wq, wkv, wo, tmask, amask, aidx, ctab, stab, coff, soff, out,
    GAIN, CT, ST, CO, SO, AIDX, TM, AM,
    X, XG, WQ, WKV, WO, ACCQ, ACCK, SSQ, QB, KV, TMR, AMR, BOWN, BFAR,
    AB, CAND, AR, SEL, AKV, MS, LS, ACC, ATT, PB, RX, RYC, RYF, SB, OB,
    ld, rx, sx, sd, loc, r0kv, r0q, r0o, s0, rz, sz, rs, ss, rm, sm,
    ra, sa, rar, sar, rak, sak, rad, sad,
    rpx, spx, rpyc, rpyf, spy, rpd, spd,
):
    ctx = lax.axis_index("ctx")
    zero = lax.axis_index("zero")
    z, xl = lax.div(ctx, 2), lax.rem(ctx, 2)
    xh, y, core = lax.div(zero, 8), lax.rem(lax.div(zero, 2), 4), lax.rem(zero, 2)
    x = 2 * xh + xl
    sib = 1 - core
    sgn = 1 - 2 * core
    home = core == xl
    away = core != xl
    pdx = 1 - 2 * xl

    def at(dx=0, dy=0, dz=0, to=None):
        nx, ny, nz = lax.rem(x + dx + 4, 4), lax.rem(y + dy + 4, 4), lax.rem(z + dz + 16, 16)
        to = core if to is None else to
        return (nz * 2 + lax.rem(nx, 2), (lax.div(nx, 2) * 4 + ny) * 2 + to)

    def remote(src, dst, send, recv, dev):
        pltpu.make_async_remote_copy(
            src_ref=src, dst_ref=dst, send_sem=send, recv_sem=recv, device_id=dev, device_id_type=MESH
        ).start()

    def wait(ref, sem):
        pltpu.make_async_copy(ref, ref, sem).wait()

    barrier = pltpu.get_barrier_semaphore()
    greet = [at(to=sib), at(dx=1), at(dx=-1), at(dx=pdx, to=sib), at(dy=1), at(dy=-1), at(dz=1), at(dz=-1)]
    for dev in greet:
        pl.semaphore_signal(barrier, inc=1, device_id=dev, device_id_type=MESH)

    loads = [
        pltpu.make_async_copy(src, dst, ld.at[n])
        for n, (src, dst) in enumerate(
            [(gain, GAIN), (ctab, CT), (stab, ST), (coff, CO), (soff, SO), (aidx, AIDX), (tmask, TM), (amask, AM)]
        )
    ]
    for copy in loads:
        copy.start()
    pl.semaphore_wait(barrier, len(greet))

    def rows(half):
        return pl.ds(half * 256, 256)

    def shard(kind, dx, dy):
        xs, ys = lax.rem(x + 4 - dx, 4), lax.rem(y + 4 - dy, 4)
        return (lax.div(xs, 2) * 4 + ys) * 2 + (core if kind == "A" else sib)

    def acts_event(event):
        kind, dx, dy, half = event
        k = shard(kind, dx, dy)
        here = X.at[k, rows(half)]
        if (kind, dx, dy) == ("A", 0, 0):
            src = acts.at[rows(half)]
        else:
            wait(here, rx.at[k, half])
            src = here
        for way in onward(*event):
            ddx, ddy = STEPS[way]
            remote(src, here, sx.at[k, half, way], rx.at[k, half], at(dx=ddx, dy=ddy))

    def acts_sent(event):
        kind, dx, dy, half = event
        k = shard(kind, dx, dy)
        for way in onward(*event):
            wait(X.at[k, rows(half)], sx.at[k, half, way])

    def piece(kind, zz, j):
        j128 = pl.multiple_of(j * 128, 128)
        if kind == 0:
            return WKV.at[zz, pl.ds(j128, 128), :]
        if kind == 1:
            return WQ.at[zz, pl.ds(j128, 128), :]
        return WO.at[zz, j]

    def kv_part(j, i):
        return WKV.at[z, pl.ds(pl.multiple_of(j * 128, 128), 128), pl.ds(pl.multiple_of(i * 128, 128), 128)]

    def zrow(d):
        return lax.rem(z - sgn * d + 32, 16)

    def local_copies():
        yield wkv, kv_part(xl, core), loc.at[0], None
        yield wq, piece(1, z, xl), loc.at[1], home
        yield wo, piece(2, z, xl), loc.at[2], home
        yield acts, X.at[zero], loc.at[3], home

    def when(cond, f):
        if cond is None:
            f()
        else:
            pl.when(cond)(f)

    for src, dst, sem, cond in local_copies():
        when(cond, lambda: pltpu.make_async_copy(src, dst, sem).start())

    @pl.when(away)
    def _():
        for half in (0, 1):
            remote(acts.at[rows(half)], X.at[zero, rows(half)], sd.at[half], rx.at[zero, half], at(to=sib))

    remote(wkv, kv_part(xl, core), s0.at[0], r0kv.at[xl, core], at(to=sib))
    remote(wkv, kv_part(xl, core), s0.at[1], r0kv.at[xl, core], at(dx=pdx))
    remote(wkv, kv_part(xl, core), s0.at[2], r0kv.at[xl, core], at(dx=pdx, to=sib))

    def share(src, kind, sem, slot):
        @pl.when(home)
        def _():
            remote(src, piece(kind, z, xl), s0.at[slot], sem.at[xl], at(to=sib))

        @pl.when(away)
        def _():
            remote(src, piece(kind, z, xl), s0.at[slot], sem.at[xl], at(dx=pdx))
            remote(src, piece(kind, z, xl), s0.at[slot + 1], sem.at[xl], at(dx=pdx, to=sib))

    remote(tmask, TMR, sm.at[0], rm.at[0], at(dx=pdx))
    remote(amask, AMR, sm.at[1], rm.at[1], at(dx=pdx))

    def z_own(kind):
        for j in (xl, 1 - xl):
            own = j is xl
            if kind == 0:
                if own:
                    pltpu.make_async_copy(wkv, kv_part(xl, core), loc.at[0]).wait()
                    wait(kv_part(xl, sib), r0kv.at[xl, sib])
                else:
                    wait(kv_part(j, 0), r0kv.at[j, 0])
                    wait(kv_part(j, 1), r0kv.at[j, 1])
            else:
                src, sem = ((wq, r0q), (wo, r0o))[kind - 1]
                if own:
                    pl.when(home)(lambda: pltpu.make_async_copy(src, piece(kind, z, xl), loc.at[kind]).wait())
                    pl.when(away)(lambda: wait(piece(kind, z, xl), sem.at[xl]))
                else:
                    wait(piece(kind, z, j), sem.at[j])
            remote(piece(kind, z, j), piece(kind, z, j), sz.at[kind, 0, j], rz.at[kind, 0, j], at(dz=sgn))

    def z_step(kind, d):
        zz = zrow(d)
        for j in (0, 1) if d < 8 else (core,):
            ref = piece(kind, zz, j)
            wait(ref, rz.at[kind, d - 1, j])
            if d < 7:
                remote(ref, ref, sz.at[kind, d, j], rz.at[kind, d, j], at(dz=sgn))
            remote(ref, ref, ss.at[kind, d - 1, j], rs.at[kind, d - 1, j], at(to=sib))
        if d == 7:
            ref = piece(kind, zz, core)
            remote(ref, ref, sz.at[kind, d, core], rz.at[kind, d, core], at(dz=sgn))

    def z_sent(kind):
        for d in range(8):
            for j in (0, 1) if d < 7 else (core,):
                wait(piece(kind, z, j), sz.at[kind, d, j])
        for d in range(1, 9):
            for j in (0, 1) if d < 8 else (core,):
                wait(piece(kind, z, j), ss.at[kind, d - 1, j])

    def z_sib(kind, d):
        for j in (0, 1) if d < 8 else (sib,):
            wait(piece(kind, zrow(-d), j), rs.at[kind, d - 1, j])

    def acts_events(lo, hi):
        @pl.when(home)
        def _():
            for event in ORDER_HOME[lo:hi]:
                acts_event(event)

        @pl.when(away)
        def _():
            for event in ORDER_AWAY[lo:hi]:
                acts_event(event)

    pl.when(home)(lambda: [acts_event(e) for e in ORDER_HOME[:2]] and None)
    share(wq, 1, r0q, 3)
    z_own(0)
    z_own(1)
    pl.when(home)(lambda: [acts_event(e) for e in ORDER_HOME[2:8]] and None)
    pl.when(away)(lambda: [acts_event(e) for e in ORDER_AWAY[:6]] and None)
    share(wo, 2, r0o, 5)
    cuts_home = [8, 13, 17, 20, 24, 28, 32]
    cuts_away = [6, 11, 16, 22, 25, 28, 32]
    for d in range(1, 7):
        z_step(0, d)
        z_step(1, d)
        if d == 4:
            z_own(2)
        if d > 4:
            z_step(2, d - 4)
        lo, hi = cuts_home[d - 1], cuts_home[d]
        pl.when(home)(lambda: [acts_event(e) for e in ORDER_HOME[lo:hi]] and None)
        lo, hi = cuts_away[d - 1], cuts_away[d]
        pl.when(away)(lambda: [acts_event(e) for e in ORDER_AWAY[lo:hi]] and None)
    for d in (7, 8):
        z_step(0, d)
        z_step(1, d)
        z_step(2, d - 4)
    pl.when(home)(lambda: pltpu.make_async_copy(acts, X.at[zero], loc.at[3]).wait())
    for d in range(1, 9):
        z_sib(0, d)
        z_sib(1, d)

    for copy in loads:
        copy.wait()
    ACCQ[...] = jnp.zeros_like(ACCQ)
    ACCK[...] = jnp.zeros_like(ACCK)
    SSQ[...] = jnp.zeros_like(SSQ)

    @pl.loop(0, 16)
    def _(k):
        v = X[k].astype(F32)
        sq = v * v
        SSQ[...] += sq[:, :128] + sq[:, 128:]
        g = GAIN[pl.ds(pl.multiple_of(k * 256, 256), 256)].astype(F32)[None, :]
        scaled = (v * g).astype(BF16)
        XG[k] = scaled
        ACCK[...] += jnp.dot(scaled, WKV[k], preferred_element_type=F32)

    inv = lax.rsqrt(jnp.sum(SSQ[...], -1, keepdims=True) * (1.0 / 4096) + 1e-5)
    block = 2 * z + core
    cb, sb = CO[pl.ds(block, 1), :], SO[pl.ds(block, 1), :]
    lane = lax.broadcasted_iota(jnp.int32, (1, 128), 1)
    cos = cb * CT[...] - sb * ST[...]
    sin = sb * CT[...] + cb * ST[...]
    sin = jnp.where(lane < 64, -sin, sin)

    def rope(v):
        return v * cos + pltpu.roll(v, 64, 1) * sin

    KV[:, :128] = rope(ACCK[:, :128] * inv).astype(BF16)
    KV[:, 128:] = (ACCK[:, 128:] * inv).astype(BF16)

    anchor = AIDX[0]
    anchor_z, anchor_core = lax.div(anchor, 2), lax.rem(anchor, 2)
    mine = pl.ds(pl.multiple_of(core * 256, 256), 256)
    remote(KV.at[pl.ds(pl.multiple_of(sib * 256, 256), 256)], AB, sa, ra, at(to=sib))
    wait(AB, ra)
    CAND[...] = jnp.where(anchor_core == core, KV[mine, :], AB[...]).reshape(16, 16, 256)

    @pl.loop(1, 16)
    def _(s):
        d = lax.rem(s + 7, 15) + 1
        to = lax.rem(z + d, 16)
        remote(CAND.at[to], AR.at[z], sar.at[d], rar.at[z], at(dz=d))

    AR[z] = CAND[z]

    @pl.loop(0, 16)
    def _(k):
        ACCQ[...] += jnp.dot(XG[k], WQ[k], preferred_element_type=F32)

    for h in (0, 1):
        q = (rope(ACCQ[:, h * 128:(h + 1) * 128] * inv) * (128 ** -0.5)).astype(BF16)
        for i in range(4):
            QB[i, h * 128:(h + 1) * 128, :] = q[i * 128:(i + 1) * 128]
    for ref, got, dst in ((TM, TMR, BOWN), (AM, AMR, BFAR)):
        wait(got, rm.at[0 if ref is TM else 1])
        seen = jnp.where(home, ref[0], got[0])
        if ref is AM:
            seen = jnp.where(block != anchor, seen, 0)
        term = jnp.where(seen == 1, 0.0, MASKED).astype(F32)
        for i in range(4):
            for j in range(4):
                dst[i, :, j * 128:(j + 1) * 128] = jnp.broadcast_to(term[i:i + 1, j:j + 1], (8, 128))

    over = (((1,), (1,)), ((), ()))
    row = lax.rem(lax.broadcasted_iota(jnp.int32, (256, 128), 0), 128)
    col = lax.broadcasted_iota(jnp.int32, (256, 128), 1)
    causal = jnp.where(col <= row, 0.0, MASKED).astype(F32)
    for i in range(4):
        n = (i + 1) * 128
        s = lax.dot_general(QB[i], KV[:n, :128], over, preferred_element_type=F32) + BOWN[i, 0:1, :n]
        last = s[:, n - 128:] + causal
        s = last if i == 0 else jnp.concatenate([s[:, :n - 128], last], 1)
        m = jnp.max(s, -1, keepdims=True)
        p = jnp.exp(s - m)
        MS[i] = jnp.broadcast_to(m, (256, 128))
        LS[i] = jnp.broadcast_to(jnp.sum(p, -1, keepdims=True), (256, 128))
        ACC[i] = jnp.dot(p.astype(BF16), KV[:n, 128:], preferred_element_type=F32)

    z_step(2, 5)
    z_step(2, 6)

    @pl.loop(1, 16)
    def _(d):
        frm = lax.rem(z + d, 16)
        wait(AR.at[frm], rar.at[frm])

    SEL[...] = AR[anchor_z]

    @pl.loop(1, 16)
    def _(s):
        d = lax.rem(s + 7, 15) + 1
        remote(SEL, AKV.at[core, z], sak.at[d], rak.at[z], at(dz=d))

    AKV[core, z] = SEL[...]
    z_step(2, 7)

    @pl.loop(1, 16)
    def _(d):
        frm = lax.rem(z + d, 16)
        wait(AKV.at[core, frm], rak.at[frm])

    remote(AKV.at[core], AKV.at[core], sad, rad, at(to=sib))
    wait(AKV.at[sib], rad)
    far = AKV[...].reshape(512, 256)
    for i in range(4):
        s = lax.dot_general(QB[i], far[:, :128], over, preferred_element_type=F32) + BFAR[i, 0:1, :]
        m0 = MS[i][:, :1]
        m = jnp.maximum(m0, jnp.max(s, -1, keepdims=True))
        p = jnp.exp(s - m)
        alpha = jnp.exp(m0 - m)
        total = LS[i][:, :1] * alpha + jnp.sum(p, -1, keepdims=True)
        o = ACC[i] * alpha + jnp.dot(p.astype(BF16), far[:, 128:], preferred_element_type=F32)
        o = (o / total).astype(BF16)
        for h in (0, 1):
            ATT[i * 128:(i + 1) * 128, h * 128:(h + 1) * 128] = o[h * 128:(h + 1) * 128]

    offsets = [0]
    for d in range(1, 8):
        offsets += [d, -d]
    offsets += [8]

    def block_of(u, half):
        return lax.rem(z + offsets[2 * u + half] + 32, 16)

    y1, y2, y3 = lax.rem(y + 1, 4), lax.rem(y + 2, 4), lax.rem(y + 3, 4)
    hr = lax.div(lax.rem(x + 1, 4), 2)
    hl = lax.div(lax.rem(x + 3, 4), 2)

    class Unit:
        def __init__(self, u):
            self.u = u
            self.xfirst = u % 2 == 0

        def xs(self, half, h):
            return PB.at[self.u, half, h] if self.xfirst else PB.at[self.u, half, h, y]

        def rxs(self, way, half):
            return RX.at[self.u, way, half] if self.xfirst else RX.at[self.u, way, half, 0]

        def ys(self, half, yy):
            return PB.at[self.u, half, xh, yy] if self.xfirst else PB.at[self.u, half, :, yy]

        def ryc(self, way):
            return RYC.at[self.u, way, 0] if self.xfirst else RYC.at[self.u, way]

        def ryf(self, way, half):
            return RYF.at[self.u, way, half, 0] if self.xfirst else RYF.at[self.u, way, half]

        def sendx(self, src, slot, dx, way, half):
            remote(src, self.rxs(way, half), spx.at[self.u, slot], rpx.at[self.u, way, half], at(dx=dx))

        def sendyc(self, src, slot, dy, way):
            remote(src, self.ryc(way), spy.at[self.u, slot], rpyc.at[self.u, way], at(dy=dy))

        def sendyf(self, src, slot, dy, way, half):
            remote(src, self.ryf(way, half), spy.at[self.u, slot], rpyf.at[self.u, way, half], at(dy=dy))

        def project(self):
            for half in (0, 1):
                b = block_of(self.u, half)
                w = jnp.concatenate([WO[b, 0], WO[b, 1]], 1)
                part = jnp.dot(ATT[...], w, preferred_element_type=F32).astype(BF16)
                PB[self.u, half] = part.reshape(2, 4, 64, 256)

        def x_begin(self):
            @pl.when(home)
            def _():
                self.sendx(self.xs(0, 1 - xh), 0, 1, 0, 0)
                self.sendx(self.xs(1, 1 - xh), 1, -1, 1, 1)

            @pl.when(away)
            def _():
                self.sendx(self.xs(1, hr), 0, 1, 0, 1)
                self.sendx(self.xs(0, hl), 1, -1, 1, 0)

        def add(self, ref, got):
            ref[...] = (ref[...].astype(F32) + got[...].astype(F32)).astype(BF16)

        def x_mid(self):
            @pl.when(away)
            def _():
                wait(self.rxs(0, 0), rpx.at[self.u, 0, 0])
                self.add(self.xs(0, hr), self.rxs(0, 0))
                self.sendx(self.xs(0, hr), 2, 1, 0, 0)
                wait(self.rxs(1, 1), rpx.at[self.u, 1, 1])
                self.add(self.xs(1, hl), self.rxs(1, 1))
                self.sendx(self.xs(1, hl), 3, -1, 1, 1)

        def total(self, ref, one, two):
            return ref[...].astype(F32) + one[...].astype(F32) + two[...].astype(F32)

        def finish(self, half, value):
            value = value.astype(BF16)
            low, high = value[:32], value[32:]
            b = pl.multiple_of(block_of(self.u, half) * 256, 256)
            out[:, pl.ds(b, 256)] = jnp.where(core == 0, low, high)
            SB[self.u, half] = jnp.where(core == 0, high, low)
            if half == 1:
                remote(SB.at[self.u], OB.at[self.u], spd.at[self.u], rpd.at[self.u], at(to=sib))

        def x_end(self):
            @pl.when(home)
            def _():
                for half in (0, 1):
                    for way in (0, 1):
                        wait(self.rxs(way, half), rpx.at[self.u, way, half])
                    value = self.total(self.xs(half, xh), self.rxs(0, half), self.rxs(1, half))
                    if self.xfirst:
                        self.xs(half, xh)[...] = value.astype(BF16)
                    else:
                        self.finish(half, value)

        def on_y(self, f):
            if self.xfirst:
                pl.when(home)(f)
            else:
                f()

        def y_begin(self):
            def f():
                self.sendyc(self.ys(0, y2), 0, 1, 0)
                self.sendyc(self.ys(1, y2), 1, -1, 1)
                self.sendyf(self.ys(1, y1), 2, 1, 0, 1)
                self.sendyf(self.ys(0, y3), 3, -1, 1, 0)

            self.on_y(f)

        def y_mid(self):
            def f():
                wait(self.ryc(0), rpyc.at[self.u, 0])
                self.add(self.ys(0, y1), self.ryc(0))
                self.sendyf(self.ys(0, y1), 4, 1, 0, 0)
                wait(self.ryc(1), rpyc.at[self.u, 1])
                self.add(self.ys(1, y3), self.ryc(1))
                self.sendyf(self.ys(1, y3), 5, -1, 1, 1)

            self.on_y(f)

        def y_end(self):
            def f():
                for half in (0, 1):
                    for way in (0, 1):
                        wait(self.ryf(way, half), rpyf.at[self.u, way, half])
                    value = self.total(self.ys(half, y), self.ryf(0, half), self.ryf(1, half))
                    if self.xfirst:
                        self.finish(half, value)
                    else:
                        self.ys(half, y)[...] = value.astype(BF16)

            self.on_y(f)

        def stage(self, s):
            if s == 0:
                self.project()
            if self.xfirst:
                parts = [[self.x_begin], [self.x_mid], [self.x_end, self.y_begin], [self.y_mid], [self.y_end]]
            else:
                parts = [[self.y_begin], [self.y_mid], [self.y_end, self.x_begin], [self.x_mid], [self.x_end]]
            for part in parts[s]:
                part()

        def sent(self):
            @pl.when(home)
            def _():
                for slot in (0, 1):
                    wait(self.rxs(0, 0), spx.at[self.u, slot])
                wait(SB.at[self.u], spd.at[self.u])

            @pl.when(away)
            def _():
                for slot in range(4):
                    wait(self.rxs(0, 0), spx.at[self.u, slot])

            def f():
                for slot in range(6):
                    wait(self.ryc(0), spy.at[self.u, slot])

            self.on_y(f)

        def collect(self):
            @pl.when(away)
            def _():
                wait(OB.at[self.u], rpd.at[self.u])
                for half in (0, 1):
                    b = pl.multiple_of(block_of(self.u, half) * 256, 256)
                    out[:, pl.ds(b, 256)] = OB[self.u, half]

    units = [Unit(u) for u in range(UNITS)]
    seen = 0
    for t in range(UNITS + 4 * LAG):
        if seen < 8:
            seen += 1
            if seen == 4:
                z_step(2, 8)
            z_sib(2, seen)
        for s in reversed(range(5)):
            u = t - s * LAG
            if 0 <= u < UNITS:
                units[u].stage(s)

    pl.when(home)(lambda: [acts_sent(e) for e in ORDER_HOME] and None)
    pl.when(away)(lambda: [acts_sent(e) for e in ORDER_AWAY] and None)

    @pl.when(away)
    def _():
        for half in (0, 1):
            wait(X.at[0, rows(half)], sd.at[half])

    for slot in range(3):
        wait(kv_part(0, 0), s0.at[slot])
    for slot, kind in ((3, 1), (5, 2)):
        wait(piece(kind, z, 0), s0.at[slot])

        @pl.when(away)
        def _():
            wait(piece(kind, z, 0), s0.at[slot + 1])

    wait(TMR, sm.at[0])
    wait(AMR, sm.at[1])
    for kind in range(3):
        z_sent(kind)
    wait(AB, sa)

    @pl.loop(1, 16)
    def _(d):
        wait(SEL, sar.at[d])
        wait(SEL, sak.at[d])

    wait(AKV.at[0], sad)
    for unit in units:
        unit.sent()
    for unit in units:
        unit.collect()


def tables():
    f = 500000.0 ** (-np.arange(64, dtype=np.float64) * 2.0 / 128)
    f = np.concatenate([f, f])
    inner = np.arange(512, dtype=np.float64)[:, None] * f
    outer = 512.0 * np.arange(32, dtype=np.float64)[:, None] * f
    return [t.astype(np.float32) for t in (np.cos(inner), np.sin(inner), np.cos(outer), np.sin(outer))]


def local(activations, norm_gain, query_weight, kv_weight, out_weight, tile_mask, anchor_mask, anchor_index):
    vmem = pl.BlockSpec(memory_space=pltpu.VMEM)
    V = pltpu.VMEM
    D = pltpu.SemaphoreType.DMA
    scratch = [
        V((4096,), BF16), V((512, 128), F32), V((512, 128), F32), V((32, 128), F32), V((32, 128), F32),
        pltpu.SMEM((1,), jnp.int32), V((1, 4, 4), jnp.int32), V((1, 4, 4), jnp.int32),
        V((16, 512, 256), BF16), V((16, 512, 256), BF16), V((16, 256, 256), BF16), V((16, 256, 256), BF16), V((16, 2, 256, 128), BF16),
        V((512, 256), F32), V((512, 256), F32), V((512, 128), F32),
        V((4, 256, 128), BF16), V((512, 256), BF16),
        V((1, 4, 4), jnp.int32), V((1, 4, 4), jnp.int32), V((4, 8, 512), F32), V((4, 8, 512), F32),
        V((256, 256), BF16), V((16, 16, 256), BF16), V((16, 16, 256), BF16), V((16, 256), BF16),
        V((2, 16, 16, 256), BF16), V((4, 256, 128), F32), V((4, 256, 128), F32), V((4, 256, 128), F32),
        V((512, 256), BF16),
        V((UNITS, 2, 2, 4, 64, 256), BF16), V((UNITS, 2, 2, 4, 64, 256), BF16),
        V((UNITS, 2, 2, 64, 256), BF16), V((UNITS, 2, 2, 2, 64, 256), BF16),
        V((UNITS, 2, 32, 256), BF16), V((UNITS, 2, 32, 256), BF16),
        D((8,)),
        D((16, 2)), D((16, 2, 4)), D((2,)), D((4,)), D((2, 2)), D((2,)), D((2,)), D((7,)),
        D((3, 8, 2)), D((3, 8, 2)), D((3, 8, 2)), D((3, 8, 2)), D((2,)), D((2,)),
        D(()), D(()), D((16,)), D((16,)), D((16,)), D((16,)), D(()), D(()),
        D((UNITS, 2, 2)), D((UNITS, 4)), D((UNITS, 2)), D((UNITS, 2, 2)), D((UNITS, 6)), D((UNITS,)), D((UNITS,)),
    ]
    return pl.pallas_call(
        body,
        out_shape=jax.ShapeDtypeStruct((32, 4096), BF16),
        in_specs=[pl.BlockSpec(memory_space=pl.ANY)] * 12,
        out_specs=vmem,
        scratch_shapes=scratch,
        compiler_params=pltpu.CompilerParams(
            collective_id=0, has_side_effects=True, vmem_limit_bytes=60 * 1024 * 1024
        ),
        name="star",
    )(
        activations, norm_gain, query_weight, kv_weight[:, 0, :], out_weight,
        tile_mask, anchor_mask, anchor_index, *[jnp.asarray(t) for t in tables()],
    )


def solution(mesh):
    placed = (
        P("ctx", "zero"), P(), P("ctx", "zero"), P("ctx", "zero", None), P("zero", "ctx"),
        P("ctx", None, None), P("ctx", None, None), P(),
    )
    return jax.shard_map(
        local, mesh=mesh, in_specs=placed, out_specs=P(("ctx", "zero"), None), check_vma=False
    )
```

```python
import functools

import numpy as np

import jax
import jax.numpy as jnp
from jax import lax
from jax.experimental import pallas as pl
from jax.experimental.pallas import tpu as pltpu
from jax.sharding import PartitionSpec as P

MESH = pl.DeviceIdType.MESH
F32 = jnp.float32
BF16 = jnp.bfloat16
MASKED = -1e30
UNITS = 8
LAG = 4

ORDER_HOME = [
    ("A", 0, 0, 0), ("A", 0, 0, 1), ("B", 0, 0, 0), ("B", 0, 0, 1), ("A", 0, 3, 0), ("A", 0, 1, 0),
    ("A", 0, 3, 1), ("A", 0, 1, 1), ("B", 0, 3, 0), ("B", 0, 1, 0), ("B", 0, 3, 1), ("B", 0, 1, 1),
    ("A", 0, 2, 0), ("A", 2, 0, 0), ("A", 2, 0, 1), ("B", 2, 0, 0), ("A", 0, 2, 1), ("B", 0, 2, 0),
    ("B", 0, 2, 1), ("B", 2, 0, 1), ("A", 2, 3, 0), ("A", 2, 1, 0), ("B", 2, 3, 0), ("B", 2, 3, 1),
    ("A", 2, 3, 1), ("A", 2, 1, 1), ("B", 2, 1, 0), ("B", 2, 1, 1), ("A", 2, 2, 0), ("A", 2, 2, 1),
    ("B", 2, 2, 0), ("B", 2, 2, 1),
]
ORDER_AWAY = [
    ("A", 1, 0, 0), ("A", 3, 0, 0), ("A", 1, 0, 1), ("A", 3, 0, 1), ("B", 1, 0, 0), ("B", 3, 0, 0),
    ("B", 1, 0, 1), ("B", 3, 0, 1), ("A", 1, 3, 0), ("A", 1, 1, 0), ("A", 3, 3, 0), ("B", 1, 3, 0),
    ("B", 3, 3, 0), ("A", 3, 1, 0), ("A", 1, 3, 1), ("B", 1, 1, 0), ("B", 3, 1, 0), ("A", 1, 1, 1),
    ("B", 3, 3, 1), ("A", 3, 3, 1), ("A", 3, 1, 1), ("B", 1, 3, 1), ("B", 3, 1, 1), ("B", 1, 1, 1),
    ("A", 1, 2, 0), ("B", 3, 2, 0), ("A", 1, 2, 1), ("B", 1, 2, 0), ("B", 3, 2, 1), ("A", 3, 2, 0),
    ("A", 3, 2, 1), ("B", 1, 2, 1),
]
STEPS = [(1, 0), (-1, 0), (0, 1), (0, -1)]
XP, XM, YP, YM = range(4)


def onward(kind, dx, dy, half):
    first, second = (dx, dy) if kind == "A" else (dy, dx)
    fp, fm, sp, sm = (XP, XM, YP, YM) if kind == "A" else (YP, YM, XP, XM)
    ways = []
    if second == 0:
        if first == 0:
            ways += [fp, fm]
        if first == 1 and half == 0:
            ways += [fp]
        if first == 3 and half == 1:
            ways += [fm]
        ways += [sp, sm]
    if second == 1 and half == 0:
        ways += [sp]
    if second == 3 and half == 1:
        ways += [sm]
    return ways


def body(
    acts, gain, wq, wkv, wo, tmask, amask, aidx, ctab, stab, coff, soff, out,
    GAIN, CT, ST, CO, SO, AIDX, TM, AM,
    X, XG, WQ, WKV, WO, ACCQ, ACCK, SSQ, QB, KV, TMR, AMR, BOWN, BFAR,
    AB, CAND, AR, SEL, AKV, MS, LS, ACC, ATT, PB, RX, RYC, RYF, SB, OB,
    ld, rx, sx, sd, loc, r0kv, r0q, r0o, s0, rz, sz, rs, ss, rm, sm,
    ra, sa, rar, sar, rak, sak, rad, sad,
    rpx, spx, rpyc, rpyf, spy, rpd, spd,
):
    ctx = lax.axis_index("ctx")
    zero = lax.axis_index("zero")
    z, xl = lax.div(ctx, 2), lax.rem(ctx, 2)
    xh, y, core = lax.div(zero, 8), lax.rem(lax.div(zero, 2), 4), lax.rem(zero, 2)
    x = 2 * xh + xl
    sib = 1 - core
    sgn = 1 - 2 * core
    home = core == xl
    away = core != xl
    pdx = 1 - 2 * xl

    def at(dx=0, dy=0, dz=0, to=None):
        nx, ny, nz = lax.rem(x + dx + 4, 4), lax.rem(y + dy + 4, 4), lax.rem(z + dz + 16, 16)
        to = core if to is None else to
        return (nz * 2 + lax.rem(nx, 2), (lax.div(nx, 2) * 4 + ny) * 2 + to)

    def remote(src, dst, send, recv, dev):
        pltpu.make_async_remote_copy(
            src_ref=src, dst_ref=dst, send_sem=send, recv_sem=recv, device_id=dev, device_id_type=MESH
        ).start()

    def wait(ref, sem):
        pltpu.make_async_copy(ref, ref, sem).wait()

    barrier = pltpu.get_barrier_semaphore()
    greet = [at(to=sib), at(dx=1), at(dx=-1), at(dx=pdx, to=sib), at(dy=1), at(dy=-1), at(dz=1), at(dz=-1)]
    for dev in greet:
        pl.semaphore_signal(barrier, inc=1, device_id=dev, device_id_type=MESH)

    loads = [
        pltpu.make_async_copy(src, dst, ld.at[n])
        for n, (src, dst) in enumerate(
            [(gain, GAIN), (ctab, CT), (stab, ST), (coff, CO), (soff, SO), (aidx, AIDX), (tmask, TM), (amask, AM)]
        )
    ]
    for copy in loads:
        copy.start()
    pl.semaphore_wait(barrier, len(greet))

    def rows(half):
        return pl.ds(half * 256, 256)

    def shard(kind, dx, dy):
        xs, ys = lax.rem(x + 4 - dx, 4), lax.rem(y + 4 - dy, 4)
        return (lax.div(xs, 2) * 4 + ys) * 2 + (core if kind == "A" else sib)

    def acts_event(event):
        kind, dx, dy, half = event
        k = shard(kind, dx, dy)
        here = X.at[k, rows(half)]
        if (kind, dx, dy) == ("A", 0, 0):
            src = acts.at[rows(half)]
        else:
            wait(here, rx.at[k, half])
            src = here
        for way in onward(*event):
            ddx, ddy = STEPS[way]
            remote(src, here, sx.at[k, half, way], rx.at[k, half], at(dx=ddx, dy=ddy))

    def acts_sent(event):
        kind, dx, dy, half = event
        k = shard(kind, dx, dy)
        for way in onward(*event):
            wait(X.at[k, rows(half)], sx.at[k, half, way])

    def piece(kind, zz, j):
        j128 = pl.multiple_of(j * 128, 128)
        if kind == 0:
            return WKV.at[zz, pl.ds(j128, 128), :]
        if kind == 1:
            return WQ.at[zz, pl.ds(j128, 128), :]
        return WO.at[zz, j]

    def kv_part(j, i):
        return WKV.at[z, pl.ds(pl.multiple_of(j * 128, 128), 128), pl.ds(pl.multiple_of(i * 128, 128), 128)]

    def zrow(d):
        return lax.rem(z - sgn * d + 32, 16)

    def local_copies():
        yield wkv, kv_part(xl, core), loc.at[0], None
        yield wq, piece(1, z, xl), loc.at[1], home
        yield wo, piece(2, z, xl), loc.at[2], home
        yield acts, X.at[zero], loc.at[3], home

    def when(cond, f):
        if cond is None:
            f()
        else:
            pl.when(cond)(f)

    for src, dst, sem, cond in local_copies():
        when(cond, lambda: pltpu.make_async_copy(src, dst, sem).start())

    @pl.when(away)
    def _():
        for half in (0, 1):
            remote(acts.at[rows(half)], X.at[zero, rows(half)], sd.at[half], rx.at[zero, half], at(to=sib))

    remote(wkv, kv_part(xl, core), s0.at[0], r0kv.at[xl, core], at(to=sib))
    remote(wkv, kv_part(xl, core), s0.at[1], r0kv.at[xl, core], at(dx=pdx))
    remote(wkv, kv_part(xl, core), s0.at[2], r0kv.at[xl, core], at(dx=pdx, to=sib))

    def share(src, kind, sem, slot):
        @pl.when(home)
        def _():
            remote(src, piece(kind, z, xl), s0.at[slot], sem.at[xl], at(to=sib))

        @pl.when(away)
        def _():
            remote(src, piece(kind, z, xl), s0.at[slot], sem.at[xl], at(dx=pdx))
            remote(src, piece(kind, z, xl), s0.at[slot + 1], sem.at[xl], at(dx=pdx, to=sib))

    remote(tmask, TMR, sm.at[0], rm.at[0], at(dx=pdx))
    remote(amask, AMR, sm.at[1], rm.at[1], at(dx=pdx))

    def z_own(kind):
        for j in (xl, 1 - xl):
            own = j is xl
            if kind == 0:
                if own:
                    pltpu.make_async_copy(wkv, kv_part(xl, core), loc.at[0]).wait()
                    wait(kv_part(xl, sib), r0kv.at[xl, sib])
                else:
                    wait(kv_part(j, 0), r0kv.at[j, 0])
                    wait(kv_part(j, 1), r0kv.at[j, 1])
            else:
                src, sem = ((wq, r0q), (wo, r0o))[kind - 1]
                if own:
                    pl.when(home)(lambda: pltpu.make_async_copy(src, piece(kind, z, xl), loc.at[kind]).wait())
                    pl.when(away)(lambda: wait(piece(kind, z, xl), sem.at[xl]))
                else:
                    wait(piece(kind, z, j), sem.at[j])
            remote(piece(kind, z, j), piece(kind, z, j), sz.at[kind, 0, j], rz.at[kind, 0, j], at(dz=sgn))

    def z_step(kind, d):
        zz = zrow(d)
        for j in (0, 1) if d < 8 else (core,):
            ref = piece(kind, zz, j)
            wait(ref, rz.at[kind, d - 1, j])
            if d < 7:
                remote(ref, ref, sz.at[kind, d, j], rz.at[kind, d, j], at(dz=sgn))
            remote(ref, ref, ss.at[kind, d - 1, j], rs.at[kind, d - 1, j], at(to=sib))
        if d == 7:
            ref = piece(kind, zz, core)
            remote(ref, ref, sz.at[kind, d, core], rz.at[kind, d, core], at(dz=sgn))

    def z_sent(kind):
        for d in range(8):
            for j in (0, 1) if d < 7 else (core,):
                wait(piece(kind, z, j), sz.at[kind, d, j])
        for d in range(1, 9):
            for j in (0, 1) if d < 8 else (core,):
                wait(piece(kind, z, j), ss.at[kind, d - 1, j])

    def z_sib(kind, d):
        for j in (0, 1) if d < 8 else (sib,):
            wait(piece(kind, zrow(-d), j), rs.at[kind, d - 1, j])

    def acts_events(lo, hi):
        @pl.when(home)
        def _():
            for event in ORDER_HOME[lo:hi]:
                acts_event(event)

        @pl.when(away)
        def _():
            for event in ORDER_AWAY[lo:hi]:
                acts_event(event)

    pl.when(home)(lambda: [acts_event(e) for e in ORDER_HOME[:2]] and None)
    share(wq, 1, r0q, 3)
    z_own(0)
    z_own(1)
    pl.when(home)(lambda: [acts_event(e) for e in ORDER_HOME[2:8]] and None)
    pl.when(away)(lambda: [acts_event(e) for e in ORDER_AWAY[:6]] and None)
    share(wo, 2, r0o, 5)
    cuts_home = [8, 12, 15, 18, 20, 24, 27, 32]
    cuts_away = [6, 10, 14, 18, 22, 25, 28, 32]
    for d in range(1, 8):
        z_step(0, d)
        z_step(1, d)
        if d == 4:
            z_own(2)
        if d > 4:
            z_step(2, d - 4)
        lo, hi = cuts_home[d - 1], cuts_home[d]
        pl.when(home)(lambda: [acts_event(e) for e in ORDER_HOME[lo:hi]] and None)
        lo, hi = cuts_away[d - 1], cuts_away[d]
        pl.when(away)(lambda: [acts_event(e) for e in ORDER_AWAY[lo:hi]] and None)
    for d in (8,):
        z_step(0, d)
        z_step(1, d)
        z_step(2, d - 4)
    pl.when(home)(lambda: pltpu.make_async_copy(acts, X.at[zero], loc.at[3]).wait())
    for d in range(1, 9):
        z_sib(0, d)
        z_sib(1, d)

    for copy in loads:
        copy.wait()
    ACCQ[...] = jnp.zeros_like(ACCQ)
    ACCK[...] = jnp.zeros_like(ACCK)
    SSQ[...] = jnp.zeros_like(SSQ)

    @pl.loop(0, 16)
    def _(k):
        v = X[k].astype(F32)
        sq = v * v
        SSQ[...] += sq[:, :128] + sq[:, 128:]
        g = GAIN[pl.ds(pl.multiple_of(k * 256, 256), 256)].astype(F32)[None, :]
        scaled = (v * g).astype(BF16)
        XG[k] = scaled
        ACCK[...] += jnp.dot(scaled, WKV[k], preferred_element_type=F32)

    inv = lax.rsqrt(jnp.sum(SSQ[...], -1, keepdims=True) * (1.0 / 4096) + 1e-5)
    block = 2 * z + core
    cb, sb = CO[pl.ds(block, 1), :], SO[pl.ds(block, 1), :]
    lane = lax.broadcasted_iota(jnp.int32, (1, 128), 1)
    cos = cb * CT[...] - sb * ST[...]
    sin = sb * CT[...] + cb * ST[...]
    sin = jnp.where(lane < 64, -sin, sin)

    def rope(v):
        return v * cos + pltpu.roll(v, 64, 1) * sin

    KV[:, :128] = rope(ACCK[:, :128] * inv).astype(BF16)
    KV[:, 128:] = (ACCK[:, 128:] * inv).astype(BF16)

    anchor = AIDX[0]
    anchor_z, anchor_core = lax.div(anchor, 2), lax.rem(anchor, 2)
    mine = pl.ds(pl.multiple_of(core * 256, 256), 256)
    remote(KV.at[pl.ds(pl.multiple_of(sib * 256, 256), 256)], AB, sa, ra, at(to=sib))
    wait(AB, ra)
    CAND[...] = jnp.where(anchor_core == core, KV[mine, :], AB[...]).reshape(16, 16, 256)

    @pl.loop(1, 16)
    def _(s):
        d = lax.rem(s + 7, 15) + 1
        to = lax.rem(z + d, 16)
        remote(CAND.at[to], AR.at[z], sar.at[d], rar.at[z], at(dz=d))

    AR[z] = CAND[z]

    @pl.loop(0, 16)
    def _(k):
        ACCQ[...] += jnp.dot(XG[k], WQ[k], preferred_element_type=F32)

    for h in (0, 1):
        q = (rope(ACCQ[:, h * 128:(h + 1) * 128] * inv) * (128 ** -0.5)).astype(BF16)
        for i in range(4):
            QB[i, h * 128:(h + 1) * 128, :] = q[i * 128:(i + 1) * 128]
    for ref, got, dst in ((TM, TMR, BOWN), (AM, AMR, BFAR)):
        wait(got, rm.at[0 if ref is TM else 1])
        seen = jnp.where(home, ref[0], got[0])
        if ref is AM:
            seen = jnp.where(block != anchor, seen, 0)
        term = jnp.where(seen == 1, 0.0, MASKED).astype(F32)
        for i in range(4):
            for j in range(4):
                dst[i, :, j * 128:(j + 1) * 128] = jnp.broadcast_to(term[i:i + 1, j:j + 1], (8, 128))

    over = (((1,), (1,)), ((), ()))
    row = lax.rem(lax.broadcasted_iota(jnp.int32, (256, 128), 0), 128)
    col = lax.broadcasted_iota(jnp.int32, (256, 128), 1)
    causal = jnp.where(col <= row, 0.0, MASKED).astype(F32)
    for i in range(4):
        n = (i + 1) * 128
        s = lax.dot_general(QB[i], KV[:n, :128], over, preferred_element_type=F32) + BOWN[i, 0:1, :n]
        last = s[:, n - 128:] + causal
        s = last if i == 0 else jnp.concatenate([s[:, :n - 128], last], 1)
        m = jnp.max(s, -1, keepdims=True)
        p = jnp.exp(s - m)
        MS[i] = jnp.broadcast_to(m, (256, 128))
        LS[i] = jnp.broadcast_to(jnp.sum(p, -1, keepdims=True), (256, 128))
        ACC[i] = jnp.dot(p.astype(BF16), KV[:n, 128:], preferred_element_type=F32)

    z_step(2, 5)
    z_step(2, 6)

    @pl.loop(1, 16)
    def _(d):
        frm = lax.rem(z + d, 16)
        wait(AR.at[frm], rar.at[frm])

    SEL[...] = AR[anchor_z]

    @pl.loop(1, 16)
    def _(s):
        d = lax.rem(s + 7, 15) + 1
        remote(SEL, AKV.at[core, z], sak.at[d], rak.at[z], at(dz=d))

    AKV[core, z] = SEL[...]
    z_step(2, 7)

    @pl.loop(1, 16)
    def _(d):
        frm = lax.rem(z + d, 16)
        wait(AKV.at[core, frm], rak.at[frm])

    remote(AKV.at[core], AKV.at[core], sad, rad, at(to=sib))
    wait(AKV.at[sib], rad)
    far = AKV[...].reshape(512, 256)
    for i in range(4):
        s = lax.dot_general(QB[i], far[:, :128], over, preferred_element_type=F32) + BFAR[i, 0:1, :]
        m0 = MS[i][:, :1]
        m = jnp.maximum(m0, jnp.max(s, -1, keepdims=True))
        p = jnp.exp(s - m)
        alpha = jnp.exp(m0 - m)
        total = LS[i][:, :1] * alpha + jnp.sum(p, -1, keepdims=True)
        o = ACC[i] * alpha + jnp.dot(p.astype(BF16), far[:, 128:], preferred_element_type=F32)
        o = (o / total).astype(BF16)
        for h in (0, 1):
            ATT[i * 128:(i + 1) * 128, h * 128:(h + 1) * 128] = o[h * 128:(h + 1) * 128]

    offsets = [0]
    for d in range(1, 8):
        offsets += [d, -d]
    offsets += [8]

    def block_of(u, half):
        return lax.rem(z + offsets[2 * u + half] + 32, 16)

    y1, y2, y3 = lax.rem(y + 1, 4), lax.rem(y + 2, 4), lax.rem(y + 3, 4)
    hr = lax.div(lax.rem(x + 1, 4), 2)
    hl = lax.div(lax.rem(x + 3, 4), 2)

    class Unit:
        def __init__(self, u):
            self.u = u
            self.xfirst = u % 2 == 0

        def xs(self, half, h):
            return PB.at[self.u, half, h] if self.xfirst else PB.at[self.u, half, h, y]

        def rxs(self, way, half):
            return RX.at[self.u, way, half] if self.xfirst else RX.at[self.u, way, half, 0]

        def ys(self, half, yy):
            return PB.at[self.u, half, xh, yy] if self.xfirst else PB.at[self.u, half, :, yy]

        def ryc(self, way):
            return RYC.at[self.u, way, 0] if self.xfirst else RYC.at[self.u, way]

        def ryf(self, way, half):
            return RYF.at[self.u, way, half, 0] if self.xfirst else RYF.at[self.u, way, half]

        def sendx(self, src, slot, dx, way, half):
            remote(src, self.rxs(way, half), spx.at[self.u, slot], rpx.at[self.u, way, half], at(dx=dx))

        def sendyc(self, src, slot, dy, way):
            remote(src, self.ryc(way), spy.at[self.u, slot], rpyc.at[self.u, way], at(dy=dy))

        def sendyf(self, src, slot, dy, way, half):
            remote(src, self.ryf(way, half), spy.at[self.u, slot], rpyf.at[self.u, way, half], at(dy=dy))

        def project(self):
            for half in (0, 1):
                b = block_of(self.u, half)
                w = jnp.concatenate([WO[b, 0], WO[b, 1]], 1)
                part = jnp.dot(ATT[...], w, preferred_element_type=F32).astype(BF16)
                PB[self.u, half] = part.reshape(2, 4, 64, 256)

        def x_begin(self):
            @pl.when(home)
            def _():
                self.sendx(self.xs(0, 1 - xh), 0, 1, 0, 0)
                self.sendx(self.xs(1, 1 - xh), 1, -1, 1, 1)

            @pl.when(away)
            def _():
                self.sendx(self.xs(1, hr), 0, 1, 0, 1)
                self.sendx(self.xs(0, hl), 1, -1, 1, 0)

        def add(self, ref, got):
            ref[...] = (ref[...].astype(F32) + got[...].astype(F32)).astype(BF16)

        def x_mid(self):
            @pl.when(away)
            def _():
                wait(self.rxs(0, 0), rpx.at[self.u, 0, 0])
                self.add(self.xs(0, hr), self.rxs(0, 0))
                self.sendx(self.xs(0, hr), 2, 1, 0, 0)
                wait(self.rxs(1, 1), rpx.at[self.u, 1, 1])
                self.add(self.xs(1, hl), self.rxs(1, 1))
                self.sendx(self.xs(1, hl), 3, -1, 1, 1)

        def total(self, ref, one, two):
            return ref[...].astype(F32) + one[...].astype(F32) + two[...].astype(F32)

        def finish(self, half, value):
            value = value.astype(BF16)
            low, high = value[:32], value[32:]
            b = pl.multiple_of(block_of(self.u, half) * 256, 256)
            out[:, pl.ds(b, 256)] = jnp.where(core == 0, low, high)
            SB[self.u, half] = jnp.where(core == 0, high, low)
            if half == 1:
                remote(SB.at[self.u], OB.at[self.u], spd.at[self.u], rpd.at[self.u], at(to=sib))

        def x_end(self):
            @pl.when(home)
            def _():
                for half in (0, 1):
                    for way in (0, 1):
                        wait(self.rxs(way, half), rpx.at[self.u, way, half])
                    value = self.total(self.xs(half, xh), self.rxs(0, half), self.rxs(1, half))
                    if self.xfirst:
                        self.xs(half, xh)[...] = value.astype(BF16)
                    else:
                        self.finish(half, value)

        def on_y(self, f):
            if self.xfirst:
                pl.when(home)(f)
            else:
                f()

        def y_begin(self):
            def f():
                self.sendyc(self.ys(0, y2), 0, 1, 0)
                self.sendyc(self.ys(1, y2), 1, -1, 1)
                self.sendyf(self.ys(1, y1), 2, 1, 0, 1)
                self.sendyf(self.ys(0, y3), 3, -1, 1, 0)

            self.on_y(f)

        def y_mid(self):
            def f():
                wait(self.ryc(0), rpyc.at[self.u, 0])
                self.add(self.ys(0, y1), self.ryc(0))
                self.sendyf(self.ys(0, y1), 4, 1, 0, 0)
                wait(self.ryc(1), rpyc.at[self.u, 1])
                self.add(self.ys(1, y3), self.ryc(1))
                self.sendyf(self.ys(1, y3), 5, -1, 1, 1)

            self.on_y(f)

        def y_end(self):
            def f():
                for half in (0, 1):
                    for way in (0, 1):
                        wait(self.ryf(way, half), rpyf.at[self.u, way, half])
                    value = self.total(self.ys(half, y), self.ryf(0, half), self.ryf(1, half))
                    if self.xfirst:
                        self.finish(half, value)
                    else:
                        self.ys(half, y)[...] = value.astype(BF16)

            self.on_y(f)

        def stage(self, s):
            if s == 0:
                self.project()
            if self.xfirst:
                parts = [[self.x_begin], [self.x_mid], [self.x_end, self.y_begin], [self.y_mid], [self.y_end]]
            else:
                parts = [[self.y_begin], [self.y_mid], [self.y_end, self.x_begin], [self.x_mid], [self.x_end]]
            for part in parts[s]:
                part()

        def sent(self):
            @pl.when(home)
            def _():
                for slot in (0, 1):
                    wait(self.rxs(0, 0), spx.at[self.u, slot])
                wait(SB.at[self.u], spd.at[self.u])

            @pl.when(away)
            def _():
                for slot in range(4):
                    wait(self.rxs(0, 0), spx.at[self.u, slot])

            def f():
                for slot in range(6):
                    wait(self.ryc(0), spy.at[self.u, slot])

            self.on_y(f)

        def collect(self):
            @pl.when(away)
            def _():
                wait(OB.at[self.u], rpd.at[self.u])
                for half in (0, 1):
                    b = pl.multiple_of(block_of(self.u, half) * 256, 256)
                    out[:, pl.ds(b, 256)] = OB[self.u, half]

    units = [Unit(u) for u in range(UNITS)]
    seen = 0
    for t in range(UNITS + 4 * LAG):
        if seen < 8:
            seen += 1
            if seen == 4:
                z_step(2, 8)
            z_sib(2, seen)
        for s in reversed(range(5)):
            u = t - s * LAG
            if 0 <= u < UNITS:
                units[u].stage(s)

    pl.when(home)(lambda: [acts_sent(e) for e in ORDER_HOME] and None)
    pl.when(away)(lambda: [acts_sent(e) for e in ORDER_AWAY] and None)

    @pl.when(away)
    def _():
        for half in (0, 1):
            wait(X.at[0, rows(half)], sd.at[half])

    for slot in range(3):
        wait(kv_part(0, 0), s0.at[slot])
    for slot, kind in ((3, 1), (5, 2)):
        wait(piece(kind, z, 0), s0.at[slot])

        @pl.when(away)
        def _():
            wait(piece(kind, z, 0), s0.at[slot + 1])

    wait(TMR, sm.at[0])
    wait(AMR, sm.at[1])
    for kind in range(3):
        z_sent(kind)
    wait(AB, sa)

    @pl.loop(1, 16)
    def _(d):
        wait(SEL, sar.at[d])
        wait(SEL, sak.at[d])

    wait(AKV.at[0], sad)
    for unit in units:
        unit.sent()
    for unit in units:
        unit.collect()


def tables():
    f = 500000.0 ** (-np.arange(64, dtype=np.float64) * 2.0 / 128)
    f = np.concatenate([f, f])
    inner = np.arange(512, dtype=np.float64)[:, None] * f
    outer = 512.0 * np.arange(32, dtype=np.float64)[:, None] * f
    return [t.astype(np.float32) for t in (np.cos(inner), np.sin(inner), np.cos(outer), np.sin(outer))]


def local(activations, norm_gain, query_weight, kv_weight, out_weight, tile_mask, anchor_mask, anchor_index):
    vmem = pl.BlockSpec(memory_space=pltpu.VMEM)
    V = pltpu.VMEM
    D = pltpu.SemaphoreType.DMA
    scratch = [
        V((4096,), BF16), V((512, 128), F32), V((512, 128), F32), V((32, 128), F32), V((32, 128), F32),
        pltpu.SMEM((1,), jnp.int32), V((1, 4, 4), jnp.int32), V((1, 4, 4), jnp.int32),
        V((16, 512, 256), BF16), V((16, 512, 256), BF16), V((16, 256, 256), BF16), V((16, 256, 256), BF16), V((16, 2, 256, 128), BF16),
        V((512, 256), F32), V((512, 256), F32), V((512, 128), F32),
        V((4, 256, 128), BF16), V((512, 256), BF16),
        V((1, 4, 4), jnp.int32), V((1, 4, 4), jnp.int32), V((4, 8, 512), F32), V((4, 8, 512), F32),
        V((256, 256), BF16), V((16, 16, 256), BF16), V((16, 16, 256), BF16), V((16, 256), BF16),
        V((2, 16, 16, 256), BF16), V((4, 256, 128), F32), V((4, 256, 128), F32), V((4, 256, 128), F32),
        V((512, 256), BF16),
        V((UNITS, 2, 2, 4, 64, 256), BF16), V((UNITS, 2, 2, 4, 64, 256), BF16),
        V((UNITS, 2, 2, 64, 256), BF16), V((UNITS, 2, 2, 2, 64, 256), BF16),
        V((UNITS, 2, 32, 256), BF16), V((UNITS, 2, 32, 256), BF16),
        D((8,)),
        D((16, 2)), D((16, 2, 4)), D((2,)), D((4,)), D((2, 2)), D((2,)), D((2,)), D((7,)),
        D((3, 8, 2)), D((3, 8, 2)), D((3, 8, 2)), D((3, 8, 2)), D((2,)), D((2,)),
        D(()), D(()), D((16,)), D((16,)), D((16,)), D((16,)), D(()), D(()),
        D((UNITS, 2, 2)), D((UNITS, 4)), D((UNITS, 2)), D((UNITS, 2, 2)), D((UNITS, 6)), D((UNITS,)), D((UNITS,)),
    ]
    return pl.pallas_call(
        body,
        out_shape=jax.ShapeDtypeStruct((32, 4096), BF16),
        in_specs=[pl.BlockSpec(memory_space=pl.ANY)] * 12,
        out_specs=vmem,
        scratch_shapes=scratch,
        compiler_params=pltpu.CompilerParams(
            collective_id=0, has_side_effects=True, vmem_limit_bytes=60 * 1024 * 1024
        ),
        name="star",
    )(
        activations, norm_gain, query_weight, kv_weight[:, 0, :], out_weight,
        tile_mask, anchor_mask, anchor_index, *[jnp.asarray(t) for t in tables()],
    )


def solution(mesh):
    placed = (
        P("ctx", "zero"), P(), P("ctx", "zero"), P("ctx", "zero", None), P("zero", "ctx"),
        P("ctx", None, None), P("ctx", None, None), P(),
    )
    return jax.shard_map(
        local, mesh=mesh, in_specs=placed, out_specs=P(("ctx", "zero"), None), check_vma=False
    )
```
